32 devices in a mesh: batch: 4 (over x, core), blk: 8 (over z, y).
Axes of the slice: x: 2, y: 2, z: 4, core: 2. Of those that a mesh axis runs over, the one named last changes fastest.
Arguments:
- latent: bfloat16 [4, 1024, 1536], P('batch', 'blk'), may hold values from -15 to 15
- time_embed: bfloat16 [4, 64], P('batch'), may hold values from -6 to 6
- text_tokens: bfloat16 [4, 77, 1280], P('batch'), may hold values from -6 to 6
- grid_shape: int32 [4, 2], P('batch'), may hold values from 8 to 112, as said below
- depth_weight: bfloat16 [9, 1536], replicated, may hold values from -5 to 5
- depth_bias: bfloat16 [1536], replicated, may hold values from -4 to 4
- widen_weight: bfloat16 [1536, 6144], P('batch'), may hold values from -0.15625 to 0.15625
- widen_bias: bfloat16 [6144], replicated, may hold values from -6 to 6
- response_gain: bfloat16 [2, 6144], replicated, may hold values from -6 to 6
- narrow_weight: bfloat16 [6144, 1536], P('batch'), may hold values from -0.078125 to 0.078125
- narrow_bias: bfloat16 [1536], replicated, may hold values from -4 to 4
- time_weight: bfloat16 [64, 3072], replicated, may hold values from -0.75 to 0.75
- time_bias: bfloat16 [3072], replicated, may hold values from -4 to 4
- text_weight: bfloat16 [1280, 1536], P('batch'), may hold values from -0.15625 to 0.15625
- text_bias: bfloat16 [1536], replicated, may hold values from -6 to 6
- project_weight: bfloat16 [1536, 4608], P('batch'), may hold values from -0.15625 to 0.15625
- project_bias: bfloat16 [3072], replicated, may hold values from -6 to 6
- output_weight: bfloat16 [1536, 1536], P('batch'), may hold values from -3 to 3
- output_bias: bfloat16 [1536], replicated, may hold values from -4 to 4
- cotangent: bfloat16 [4, 1024, 1536], P('batch', 'blk'), may hold values from -6 to 6
Outputs:
- block_output: bfloat16 [4, 1024, 1536], P('batch', 'blk')
- latent_grad: bfloat16 [4, 1024, 1536], P('batch', 'blk')
- depth_weight_grad: float32 [9, 1536], replicated
- depth_bias_grad: float32 [1536], replicated
- widen_weight_grad: float32 [1536, 6144], P('batch', 'blk')
- widen_bias_grad: float32 [6144], replicated
- response_gain_grad: float32 [2, 6144], replicated
- narrow_weight_grad: float32 [6144, 1536], P('batch', 'blk')
- narrow_bias_grad: float32 [1536], replicated
- time_weight_grad: float32 [64, 3072], replicated
- time_bias_grad: float32 [3072], replicated
- text_weight_grad: float32 [1280, 1536], P('batch', 'blk')
- text_bias_grad: float32 [1536], replicated
- project_weight_grad: float32 [1536, 4608], P('batch', 'blk')
- project_bias_grad: float32 [3072], replicated
- output_weight_grad: float32 [1536, 1536], P('batch', 'blk')
- output_bias_grad: float32 [1536], replicated
The draws below stay inside these ranges and needn't reach their ends.
Inputs may be any that keep to these rules, and one draw needn't show every extreme that they name: `grid_shape`: column 0 is a latent's width w, from 56 to 112, and column 1 its height h = 896 // w; both ends of the widths occur in every draw.
All inputs are finite; a program needn't handle non-finite values.
Results may differ from the reference program's by a relative error of at most 0.017.
Values may be sent and summed in bfloat16 or wider, within the bound.
No kernel may reach another device: no remote copies, remote signals or barrier semaphores. Data moves between devices by JAX's collectives and lax.ppermute only.
A program may use at most 384 MiB of HBM per device.

```python
import jax
import jax.numpy as jnp
from jax import lax

HEADS = 24
HDIM = 64
C = 1536
FF = 6144
CLIP = 1280
TEXT = 77
RDIM = 64
ROWS_DEV = 128
SEQ = 1024
ITEMS = 4
WIDE = 112


def draw_grid_shape(key, part):
    narrow_width = WIDE // 2
    widths = jax.random.randint(key, (ITEMS,), narrow_width, WIDE + 1, dtype=jnp.int32)
    widths = widths.at[0].set(WIDE).at[1].set(narrow_width)
    order = jax.random.permutation(jax.random.fold_in(key, 7), ITEMS)
    widths = widths[order]
    heights = SEQ * 7 // 8 // widths
    return jnp.stack([widths, heights], axis=1).astype(jnp.int32)


def draw_latent(key, part):
    noise_key = jax.random.fold_in(key, 11)
    region_key = jax.random.fold_in(key, 13)
    noise = jnp.clip(jax.random.normal(noise_key, (ITEMS, SEQ, C), jnp.float32), -6.0, 6.0)
    regions = jnp.clip(jax.random.normal(region_key, (ITEMS, SEQ // ROWS_DEV, C), jnp.float32), -3.0, 3.0)
    pattern = jnp.repeat(regions, ROWS_DEV, axis=1)
    position = jnp.arange(SEQ, dtype=jnp.float32) / SEQ
    strength = 0.5 + 2.5 * position
    return (noise + strength[None, :, None] * pattern).astype(jnp.bfloat16)


def draw_response_gain(key, part):
    scale_key = jax.random.fold_in(key, 17)
    shift_key = jax.random.fold_in(key, 19)
    gamma = jnp.clip(1.5 * jax.random.normal(scale_key, (FF,), jnp.float32), -6.0, 6.0)
    beta = jnp.clip(0.3 * jax.random.normal(shift_key, (FF,), jnp.float32), -6.0, 6.0)
    return jnp.stack([gamma, beta], axis=0).astype(jnp.bfloat16)


def steps_of(own_key, extent, cuts, smallest, high):
    loudness, own = 1.0, jax.random.fold_in(own_key, 6)
    for dim, shards_of in cuts:
        draws = jnp.exp(jax.random.uniform(jax.random.fold_in(own, dim), (shards_of,), jnp.float32, smallest / len(cuts), high / len(cuts)))
        loudness = loudness * jnp.repeat(draws, extent[dim] // shards_of).reshape([-1 if axis == dim else 1 for axis in range(len(extent))])
    return loudness


def gaussian(rng, extent, width, reach, cuts=(), kind=jnp.bfloat16):
    drawn = width * jax.random.normal(rng, extent, jnp.float32)
    if cuts:
        drawn = drawn * steps_of(rng, extent, cuts, -0.22, 0.18)
    return jnp.clip(drawn, -reach, reach).astype(kind)


def setup_inputs(seed: int = 0) -> dict:
    key_of = jax.random.split(jax.random.key(seed), 21)
    return {
        "latent": draw_latent(jax.random.fold_in(key_of[20], 71), 0),
        "time_embed": gaussian(key_of[1], (ITEMS, RDIM), 1.0, 6.0, ((0, 4),)),
        "text_tokens": gaussian(key_of[2], (ITEMS, TEXT, CLIP), 1.0, 6.0, ((0, 4),)),
        "grid_shape": draw_grid_shape(jax.random.fold_in(key_of[20], 71), 0),
        "depth_weight": gaussian(key_of[4], (9, C), 0.33, 5.0),
        "depth_bias": gaussian(key_of[5], (C,), 0.3, 4.0),
        "widen_weight": gaussian(key_of[6], (C, FF), C ** -0.5, 0.15625, ((0, 4),)),
        "widen_bias": gaussian(key_of[7], (FF,), 0.5, 6.0),
        "response_gain": draw_response_gain(jax.random.fold_in(key_of[20], 71), 0),
        "narrow_weight": gaussian(key_of[9], (FF, C), FF ** -0.5, 0.078125, ((0, 4),)),
        "narrow_bias": gaussian(key_of[10], (C,), 0.3, 4.0),
        "time_weight": gaussian(key_of[11], (RDIM, 2 * C), 0.05, 0.75),
        "time_bias": gaussian(key_of[12], (2 * C,), 0.3, 4.0),
        "text_weight": gaussian(key_of[13], (CLIP, C), CLIP ** -0.5, 0.15625, ((0, 4),)),
        "text_bias": gaussian(key_of[14], (C,), 0.5, 6.0),
        "project_weight": gaussian(key_of[15], (C, 3 * C), C ** -0.5, 0.15625, ((0, 4),)),
        "project_bias": gaussian(key_of[16], (2 * C,), 0.5, 6.0),
        "output_weight": gaussian(key_of[17], (C, C), 4 ** -0.5, 3.0, ((0, 4),)),
        "output_bias": gaussian(key_of[18], (C,), 0.3, 4.0),
        "cotangent": gaussian(key_of[19], (ITEMS, SEQ, C), 1.0, 6.0, ((0, 4), (1, 8))),
    }


@jax.custom_vjp
def low(v):
    return lax.optimization_barrier(v.astype(jnp.bfloat16)).astype(jnp.float32)

@jax.custom_vjp
def low_back(v):
    return v

def low_keep(v):
    return (low(v), None)

def low_pass(kept, grad):
    return (grad,)

def back_keep(v):
    return (v, None)

def back_low(kept, grad):
    return (low(grad),)
low.defvjp(low_keep, low_pass)
low_back.defvjp(back_keep, back_low)
highest = lax.Precision.HIGHEST
norm_eps = 1e-06
masked_score = -1e+30

def product(left, right):
    return jnp.dot(left, right, precision=highest, preferred_element_type=jnp.float32)

def row_norm(field_rows):
    average = lax.optimization_barrier(jnp.mean(field_rows, axis=-1, keepdims=True))
    centred = field_rows - average
    spread = lax.optimization_barrier(jnp.mean(centred * centred, axis=-1, keepdims=True))
    return centred * lax.rsqrt(spread + norm_eps)

def tap_valid(row_index, grid_width, height, step_row, step_col):
    row_of = row_index // grid_width
    col_of = row_index % grid_width
    inside = (row_index >= 0) & (row_index < grid_width * height)
    return inside & (row_of + step_row >= 0) & (row_of + step_row < height) & (col_of + step_col >= 0) & (col_of + step_col < grid_width)

def depthwise(extended, grid_width, height, row_index, depth_taps, depth_shift, margin):
    row_total = row_index.shape[0]
    summed = jnp.zeros((row_total, extended.shape[1]), jnp.float32)
    for tap_index in range(9):
        step_row = tap_index // 3 - 1
        step_col = tap_index % 3 - 1
        offset = (margin + step_row * grid_width + step_col).astype(jnp.int32)
        shifted = lax.dynamic_slice_in_dim(extended, offset, row_total, 0).astype(jnp.float32)
        valid_tap = tap_valid(row_index, grid_width, height, step_row, step_col)
        summed = summed + jnp.where(valid_tap[:, None], shifted, 0.0) * depth_taps[tap_index]
    inside = (row_index >= 0) & (row_index < grid_width * height)
    return jnp.where(inside[:, None], summed + depth_shift, 0.0)

def attend_rows(query_block, key_rows, value_rows, key_live):
    scores = jnp.einsum('qhd,khd->hqk', query_block, key_rows, precision=highest) * 0.125
    scores = low_back(scores)
    scores = jnp.where(key_live[None, None, :], scores, masked_score)
    row_peak = lax.optimization_barrier(jnp.max(scores, axis=-1, keepdims=True))
    exponent = jnp.exp(scores - row_peak)
    shares = exponent / lax.optimization_barrier(jnp.sum(exponent, axis=-1, keepdims=True))
    return jnp.einsum('hqk,khd->qhd', low(shares), value_rows, precision=highest)

def item_forward(params, latent, text_rows, time_row, grid_width, height):
    depth_weight, depth_bias, widen_weight, widen_bias, response_gain, narrow_weight, narrow_bias, time_weight, time_bias, text_weight, text_bias, project_weight, project_bias, output_weight, output_bias = params
    row_total = latent.shape[0]
    row_index = jnp.arange(row_total, dtype=jnp.int32)
    inside = row_index < grid_width * height
    keep_rows = inside.astype(jnp.float32)[:, None]
    margin = WIDE + 1
    extended = jnp.pad(latent, ((margin, margin), (0, 0)))
    conved = depthwise(extended, grid_width, height, row_index, depth_weight, depth_bias, margin)
    pre_act = low_back(product(low(row_norm(conved)), widen_weight) + widen_bias)
    hidden = jax.nn.gelu(pre_act, approximate=False) * keep_rows
    magnitude = jnp.sqrt(lax.optimization_barrier(jnp.sum(hidden * hidden, axis=0)) + norm_eps)
    relative = magnitude / (jnp.mean(magnitude) + norm_eps)
    grn_out = response_gain[0] * (hidden * relative) + response_gain[1] + hidden
    branch = low_back(product(low(grn_out), narrow_weight) + narrow_bias)
    after_res = latent + keep_rows * branch
    shift_scale = product(time_row[None, :], time_weight)[0] + time_bias
    modulated = after_res * (1.0 + shift_scale[:C]) + shift_scale[C:]
    normed = low(row_norm(modulated))
    text_in = low(low_back(product(low(jax.nn.silu(text_rows)), text_weight) + text_bias))
    kv_in = jnp.concatenate([normed, text_in], axis=0)
    queries = low(low_back(product(normed, project_weight[:, :C]) + project_bias[:C]))
    key_rows = low(low_back(product(kv_in, project_weight[:, C:2 * C])))
    value_rows = low(low_back(product(kv_in, project_weight[:, 2 * C:]) + project_bias[C:]))
    key_live = jnp.concatenate([inside, jnp.ones((TEXT,), dtype=bool)])
    block_rows = min(512, row_total)
    query_blocks = queries.reshape(row_total // block_rows, block_rows, HEADS, HDIM)
    keys_split = key_rows.reshape(-1, HEADS, HDIM)
    values_split = value_rows.reshape(-1, HEADS, HDIM)
    attend = jax.checkpoint(attend_rows)
    attended = lax.map(lambda q_block: attend(q_block, keys_split, values_split, key_live), query_blocks)
    attended = low(low_back(attended.reshape(row_total, C)))
    att_out = low_back(product(attended, output_weight) + output_bias)
    return modulated + att_out

def reference(latent, time_embed, text_tokens, grid_shape, depth_weight, depth_bias, widen_weight, widen_bias, response_gain, narrow_weight, narrow_bias, time_weight, time_bias, text_weight, text_bias, project_weight, project_bias, output_weight, output_bias, cotangent):
    params = tuple((weight.astype(jnp.float32) for weight in (depth_weight, depth_bias, widen_weight, widen_bias, response_gain, narrow_weight, narrow_bias, time_weight, time_bias, text_weight, text_bias, project_weight, project_bias, output_weight, output_bias)))
    zero_grads = tuple((jnp.zeros_like(weight) for weight in params))

    def one_item(running, item_slice):
        lat_item, time_item, text_item, grid_item, cot_item = item_slice

        def forward(param_tree, lat_in):
            return item_forward(param_tree, lat_in, text_item.astype(jnp.float32), time_item.astype(jnp.float32), grid_item[0], grid_item[1])
        result, pullback = jax.vjp(forward, params, lat_item.astype(jnp.float32))
        param_grads, lat_grad = pullback(cot_item.astype(jnp.float32))
        running = tuple((current + addend for current, addend in zip(running, param_grads)))
        return (running, (result.astype(jnp.bfloat16), lat_grad.astype(jnp.bfloat16)))
    grad_sums, (outputs, lat_grads) = lax.scan(one_item, zero_grads, (latent, time_embed, text_tokens, grid_shape, cotangent))
    return (outputs, lat_grads, grad_sums[0], grad_sums[1], grad_sums[2], grad_sums[3], grad_sums[4], grad_sums[5], grad_sums[6], grad_sums[7], grad_sums[8], grad_sums[9], grad_sums[10], grad_sums[11], grad_sums[12], grad_sums[13], grad_sums[14])
```

```python
import jax
import jax.numpy as jnp
from jax import lax
from jax.sharding import PartitionSpec as P

HEADS = 24
HDIM = 64
WIDE = 112

norm_eps = 1e-06
masked_score = -1e30
f32 = jnp.float32
bf16 = jnp.bfloat16


def mm(left, right, dims):
    return lax.dot_general(left, right, (dims, ((), ())), preferred_element_type=f32)


def swap(cells, axis, distance):
    count = lax.axis_size(axis)
    return lax.ppermute(cells, axis, [(i, i ^ distance) for i in range(count)])


def bits_of(count):
    return [1 << n for n in range(count.bit_length() - 1)]


def gather_batch(cells):
    held = {0: cells}
    for bit in reversed(bits_of(lax.axis_size("batch"))[1:]):
        for place in list(held):
            held[place ^ bit] = swap(held[place], "batch", bit)
    for place in list(held):
        held[place ^ 1] = swap(held[place], "batch", 1)
    return [held[d] for d in range(len(held))]


def scatter_batch(parts):
    held = dict(enumerate(parts))
    for bit in bits_of(lax.axis_size("batch")):
        held = {
            place: cells + swap(held[place ^ bit].astype(bf16), "batch", bit).astype(f32)
            for place, cells in held.items()
            if not place & bit
        }
    return held[0]


def tree_sum(pieces):
    pieces = list(pieces)
    while len(pieces) > 1:
        pieces = [pieces[i] + pieces[i + 1] for i in range(0, len(pieces), 2)]
    return pieces[0]


def sum_over(cells, axis):
    count = lax.axis_size(axis)
    if axis == "blk" and count == 8:
        cells = cells + swap(cells, axis, 1)
        return tree_sum([cells] + [swap(cells, axis, d) for d in (2, 4, 6)])
    if count <= 4:
        return tree_sum([cells] + [swap(cells, axis, d) for d in range(1, count)])
    for bit in bits_of(count):
        cells = cells + swap(cells, axis, bit)
    return cells


def take(cells, place, axis=0):
    return lax.dynamic_index_in_dim(cells, place, axis, keepdims=False)


def put(cells, piece, place):
    return lax.dynamic_update_index_in_dim(cells, piece, place, 0)


def scatter_rows(shards):
    count = shards.shape[0]
    if count != 8:
        return lax.psum_scatter(shards, "blk", scatter_dimension=0, tiled=False).astype(f32)
    place = lax.axis_index("blk")
    depth, side = place // 2, place % 2
    pairs = shards.reshape((4, 2) + shards.shape[1:])
    other = swap(take(pairs, 1 - side, 1), "blk", 1)
    halves = (take(pairs, side, 1).astype(f32) + other.astype(f32)).astype(bf16)
    up = down = None
    for step in (1, 2, 3):
        rise = take(halves, jnp.clip(depth + 4 - step, 0, 3))
        fall = take(halves, jnp.clip(depth - 4 + step, 0, 3))
        if step > 1:
            rise = (rise.astype(f32) + up.astype(f32)).astype(bf16)
            fall = (fall.astype(f32) + down.astype(f32)).astype(bf16)
        senders = [(2 * d + s, 2 * d + 2 + s) for d in range(step) for s in range(2)]
        up = lax.ppermute(rise, "blk", senders)
        down = lax.ppermute(fall, "blk", [(7 - i, 7 - j) for i, j in senders])
    return take(halves, depth).astype(f32) + up.astype(f32) + down.astype(f32)


def row_norm(field_rows):
    average = jnp.mean(field_rows, axis=-1, keepdims=True)
    centred = field_rows - average
    spread = jnp.mean(centred * centred, axis=-1, keepdims=True)
    inverse = lax.rsqrt(spread + norm_eps)
    return (centred * inverse, inverse)


def row_norm_back(normed, inverse, upstream):
    first_mean = jnp.mean(upstream, axis=-1, keepdims=True)
    second_mean = jnp.mean(upstream * normed, axis=-1, keepdims=True)
    return inverse * (upstream - first_mean - normed * second_mean)


def halo(cells, margin):
    count = lax.axis_size("blk")
    head = cells[:margin]
    tail = cells[cells.shape[0] - margin :]
    before = lax.ppermute(tail, "blk", [(i, i + 1) for i in range(count - 1)])
    after = lax.ppermute(head, "blk", [(i + 1, i) for i in range(count - 1)])
    return jnp.concatenate([before, cells, after], axis=0)


def attend(queries, keys, values, grad_heads, live):
    scores = mm(queries, keys, ((1,), (1,))) * 0.125
    scores = jnp.where(live, scores, masked_score)
    raised = jnp.exp(scores - jnp.max(scores, axis=1, keepdims=True))
    shares = raised / jnp.sum(raised, axis=1, keepdims=True)
    shares_low = shares.astype(bf16)
    attended = mm(shares_low, values, ((1,), (0,)))
    delta = jnp.sum(grad_heads.astype(f32) * attended, axis=1, keepdims=True)
    dshares = mm(grad_heads, values, ((1,), (1,)))
    dscores = (shares * (dshares - delta)).astype(bf16)
    return (
        attended,
        mm(dscores, keys, ((1,), (0,))) * 0.125,
        mm(dscores, queries, ((0,), (0,))) * 0.125,
        mm(shares_low, grad_heads, ((0,), (0,))),
    )


def colour(sources, targets, degree):
    left = list(range(len(sources)))
    rounds = []
    for _ in range(degree):
        owner = {}

        def grow(node, seen):
            for edge in left:
                if sources[edge] != node or targets[edge] in seen:
                    continue
                seen.add(targets[edge])
                taken = owner.get(targets[edge])
                if taken is None or grow(sources[taken], seen):
                    owner[targets[edge]] = edge
                    return True
            return False

        for node in range(max(sources) + 1):
            grow(node, set())
        rounds.append(sorted(owner.values()))
        left = [edge for edge in left if edge not in set(rounds[-1])]
    return rounds


def on_device(
    latent,
    time_embed,
    text_tokens,
    grid_shape,
    depth_weight,
    depth_bias,
    widen_weight,
    widen_bias,
    response_gain,
    narrow_weight,
    narrow_bias,
    time_weight,
    time_bias,
    text_weight,
    text_bias,
    project_weight,
    project_bias,
    output_weight,
    output_bias,
    cotangent,
):
    _, rows, channels = latent.shape
    batch, blk = lax.axis_size("batch"), lax.axis_size("blk")
    bi, ki = lax.axis_index("batch"), lax.axis_index("blk")
    units = widen_weight.shape[1]
    mine = units // batch
    wide_rows = channels // batch
    own_heads = HEADS // batch
    per = -(-batch * own_heads // blk)
    groups = own_heads // per
    span = per * HDIM
    used = batch * groups
    clip_rows = text_weight.shape[0]
    text_count = text_tokens.shape[1]
    ring = blk // batch
    lat = latent[0]
    cot = cotangent[0]

    facts = jnp.concatenate(
        [
            grid_shape.astype(f32),
            time_embed.astype(f32),
            jnp.zeros((1, 126 - time_embed.shape[1]), f32),
        ],
        axis=1,
    )
    facts = gather_batch(facts)
    pixels = jnp.stack([cells[0, 0] * cells[0, 1] for cells in facts])
    times = [cells[0, 2 : 2 + time_embed.shape[1]] for cells in facts]

    margin = WIDE + 1
    source_ext = halo(lat, margin)

    wide = jnp.zeros((batch, wide_rows, mine), bf16)
    for d in range(batch):
        piece = lax.dynamic_slice(widen_weight, (0, (bi ^ d) * mine), (wide_rows, mine))
        if d:
            piece = swap(piece, "batch", d)
        wide = put(wide, piece, bi ^ d)
    wide = wide.reshape(channels, mine)

    grid_w = grid_shape[0, 0]
    grid_h = grid_shape[0, 1]
    row_index = ki * rows + jnp.arange(rows, dtype=jnp.int32)
    row_of = jnp.floor((row_index.astype(f32) + 0.5) / grid_w.astype(f32)).astype(jnp.int32)
    col_of = row_index - row_of * grid_w
    inside = row_index < grid_w * grid_h
    keep_own = inside.astype(f32)[:, None]

    def valid(step_row, step_col):
        return (
            inside
            & (row_of + step_row >= 0)
            & (row_of + step_row < grid_h)
            & (col_of + step_col >= 0)
            & (col_of + step_col < grid_w)
        )[:, None]

    taps = [(tap // 3 - 1, tap % 3 - 1) for tap in range(9)]
    depth_taps = depth_weight.astype(f32)

    def window(ext, step_row, step_col):
        start = margin + step_row * grid_w + step_col
        moved = lax.dynamic_slice_in_dim(ext, start, rows, 0).astype(f32)
        return jnp.where(valid(step_row, step_col), moved, 0.0)

    conved = jnp.zeros((rows, channels), f32)
    for tap, (step_row, step_col) in enumerate(taps):
        conved = conved + window(source_ext, step_row, step_col) * depth_taps[tap]
    conved = jnp.where(inside[:, None], conved + depth_bias.astype(f32), 0.0)
    normed_one, inverse_one = row_norm(conved)
    first_in = jnp.concatenate(gather_batch(normed_one.astype(bf16)), axis=0)

    keep = (row_index.astype(f32)[None, :] < pixels[:, None]).astype(f32).reshape(-1, 1)
    widen_shift = lax.dynamic_slice(widen_bias, (bi * mine,), (mine,)).astype(f32)
    pre_act = mm(first_in, wide, ((1,), (0,))) + widen_shift
    gauss = 0.5 * (1.0 + lax.erf(pre_act * (0.5**0.5)))
    hidden = pre_act * gauss * keep

    def per_latent(cells):
        return jnp.sum(cells.reshape(batch, rows, -1), axis=1)

    order = bi ^ jnp.arange(batch, dtype=jnp.int32)
    place_of = (order[:, None] == jnp.arange(batch, dtype=jnp.int32)[None, :]).astype(f32)

    def total_over_units(cells):
        own = jnp.sum(cells, axis=1)
        natural = jnp.sum(place_of * own[:, None], axis=0)
        summed = sum_over(jnp.broadcast_to(natural[:, None], (batch, 128)), "batch")[:, 0]
        return jnp.sum(place_of * summed[None, :], axis=1)[:, None]

    squares = sum_over(per_latent(hidden * hidden), "blk")
    magnitude = jnp.sqrt(squares + norm_eps)
    mean_mag = total_over_units(magnitude) / units + norm_eps
    relative = magnitude / mean_mag

    def spread(cells):
        return jnp.repeat(cells, rows, axis=0)

    gains = lax.dynamic_slice(response_gain, (0, bi * mine), (2, mine)).astype(f32)
    second_in = (gains[0] * (hidden * spread(relative)) + gains[1] + hidden).astype(bf16)
    branch_part = mm(second_in, narrow_weight, ((1,), (0,)))

    def split(cells):
        return [cells[d * rows : (d + 1) * rows] for d in range(batch)]

    branch = scatter_batch(split(branch_part)) + narrow_bias.astype(f32)
    after_res = lat.astype(f32) + keep_own * branch
    shift_scale = mm(time_embed, time_weight, ((1,), (0,))) + time_bias.astype(f32)
    scale_part = 1.0 + shift_scale[:, :channels]
    modulated = after_res * scale_part + shift_scale[:, channels:]
    normed_two, inverse_two = row_norm(modulated)
    attn_in = jnp.concatenate(gather_batch(normed_two.astype(bf16)), axis=0)

    def project_piece(member):
        pieces = [
            lax.dynamic_slice(
                project_weight,
                (0, third * channels + member * wide_rows + group * span),
                (wide_rows, span),
            )
            for group in range(groups)
            for third in range(3)
        ]
        return jnp.concatenate(pieces, axis=1)

    project = jnp.zeros((batch, wide_rows, 3 * wide_rows), bf16)
    for d in range(batch):
        piece = project_piece(bi ^ d)
        if d:
            piece = swap(piece, "batch", d)
        project = put(project, piece, bi ^ d)
    project = project.reshape(channels, 3 * wide_rows)
    shift_q = lax.dynamic_slice(project_bias, (bi * wide_rows,), (wide_rows,)).astype(f32)
    shift_v = lax.dynamic_slice(project_bias, (channels + bi * wide_rows,), (wide_rows,)).astype(
        f32
    )
    project_shift = jnp.concatenate(
        [
            cells
            for group in range(groups)
            for cells in (
                shift_q[group * span : (group + 1) * span],
                jnp.zeros((span,), f32),
                shift_v[group * span : (group + 1) * span],
            )
        ]
    )

    def slot_of(member):
        return jnp.minimum(member // groups, batch - 1), member % groups

    def to_heads(cells):
        received = []
        for e in range(blk):
            item, group = slot_of(ki ^ e)
            piece = take(take(cells, group), item ^ bi)
            received.append(swap(piece, "blk", e) if e else piece)
        return jnp.concatenate(received, axis=0)

    def to_rows(cells):
        held = jnp.zeros((used + 1, rows, cells.shape[1]), cells.dtype)
        for e in range(blk):
            piece = cells[e * rows : (e + 1) * rows]
            if e:
                piece = swap(piece, "blk", e)
            item, group = slot_of(ki ^ e)
            slot = jnp.where((ki ^ e) < used, group * batch + (item ^ bi), used)
            held = put(held, piece, slot)
        return held[:used].reshape(groups, batch, rows, cells.shape[1])

    item, group = slot_of(ki)
    working = (ki < used).astype(f32)

    soft = jax.nn.silu(text_tokens[0].astype(f32)).astype(bf16)
    soft_mine = []
    for d in range(batch):
        piece = lax.dynamic_slice(soft, (0, (bi ^ d) * clip_rows), (text_count, clip_rows))
        soft_mine.append(swap(piece, "batch", d) if d else piece)
    soft_mine = jnp.stack(soft_mine)
    text_sum = mm(take(soft_mine, item ^ bi), text_weight, ((1,), (0,)))
    for bit in bits_of(batch):
        text_sum = text_sum + swap(text_sum, "batch", bit)
    text_feat = (text_sum + text_bias.astype(f32)).astype(bf16)
    text_proj = (mm(text_feat, project, ((1,), (0,))) + project_shift).astype(bf16)
    text_proj = jnp.stack(
        [text_proj[:, g * 3 * span : (g + 1) * 3 * span] for g in range(groups)]
    )
    text_proj = take(text_proj, group)

    cot_rows = jnp.concatenate(gather_batch(cot), axis=0)
    grad_heads = jnp.stack(
        [
            mm(cot_rows, output_weight[g * span : (g + 1) * span], ((1,), (1,))).astype(bf16)
            for g in range(groups)
        ]
    ).reshape(groups, batch, rows, span)
    grad_heads = to_heads(grad_heads)

    projected = (mm(attn_in, project, ((1,), (0,))) + project_shift).astype(bf16)
    projected = jnp.stack(
        [projected[:, g * 3 * span : (g + 1) * 3 * span] for g in range(groups)]
    ).reshape(groups, batch, rows, 3 * span)
    projected = to_heads(projected)

    own_pixels = take(pixels, item ^ bi)
    seq_rows = jnp.concatenate(
        [((ki ^ e) * rows).astype(f32) + jnp.arange(rows, dtype=f32) for e in range(blk)]
        + [jnp.full((text_count,), -1.0, f32)]
    )
    live = (seq_rows < own_pixels)[None, :]
    keys = jnp.concatenate([projected[:, span : 2 * span], text_proj[:, span : 2 * span]], axis=0)
    values = jnp.concatenate([projected[:, 2 * span :], text_proj[:, 2 * span :]], axis=0)
    heads = []
    for head in range(per):
        cut = slice(head * HDIM, (head + 1) * HDIM)
        heads.append(
            attend(projected[:, cut], keys[:, cut], values[:, cut], grad_heads[:, cut], live)
        )
    attended, dq, dk, dv = (jnp.concatenate(cells, axis=1).astype(bf16) for cells in zip(*heads))
    seq = blk * rows
    dqkv = to_rows(jnp.concatenate([dq, dk[:seq], dv[:seq]], axis=1))
    dqkv = jnp.concatenate(
        [dqkv[g].reshape(batch * rows, 3 * span) for g in range(groups)], axis=1
    )
    attended = to_rows(attended)
    attended = jnp.concatenate(
        [attended[g].reshape(batch * rows, span) for g in range(groups)], axis=1
    )

    dnormed_two = scatter_batch(split(mm(dqkv, project, ((1,), (1,)))))

    att_out = scatter_batch(split(mm(attended, output_weight, ((1,), (0,)))))
    block_output = (modulated + att_out + output_bias.astype(f32)).astype(bf16)
    upstream = cot.astype(f32)
    output_grad = mm(cot_rows, attended, ((0,), (0,))).astype(bf16)
    output_sum = scatter_rows(output_grad.reshape(blk, channels // blk, wide_rows)).T

    dtext_low = jnp.concatenate([jnp.zeros((text_count, span), bf16), dk[seq:], dv[seq:]], axis=1)
    dtext_low = (dtext_low.astype(f32) * working).astype(bf16)
    dtext_cols = jnp.concatenate(
        [
            jnp.where(group == g, dtext_low, jnp.zeros_like(dtext_low))
            for g in range(groups)
        ],
        axis=1,
    )
    dtext_part = mm(dtext_cols, project, ((1,), (1,)))
    natural_items = jnp.arange(batch, dtype=jnp.int32)
    if blk == 2 * batch and groups == 2:
        part = dtext_part
        for axis, distance in (("blk", 1), ("batch", 1), ("batch", 2)):
            low = part.astype(bf16)
            part = low.astype(f32) + swap(low, axis, distance).astype(f32)
        low = part.astype(bf16)
        dtext_all = jnp.zeros((batch, text_count, channels), bf16)
        for d in range(batch):
            piece = swap(low, "blk", 2 * d) if d else low
            dtext_all = put(dtext_all, piece, item ^ d)
    else:
        placed = (natural_items == item).astype(f32)[:, None, None] * dtext_part[None]
        dtext_all = lax.psum(placed, ("batch", "blk")).astype(bf16)
    text_bias_sum = jnp.sum(dtext_all.astype(f32), axis=(0, 1))
    dtext_cut = lax.dynamic_slice(
        dtext_all, (0, 0, ki * (channels // blk)), (batch, text_count, channels // blk)
    )
    soft_natural = jnp.stack([take(soft_mine, l ^ bi) for l in range(batch)])
    text_sum_grad = mm(
        soft_natural.reshape(batch * text_count, clip_rows),
        dtext_cut.reshape(batch * text_count, channels // blk),
        ((0,), (0,)),
    )

    project_grad = mm(attn_in, dqkv, ((0,), (0,))) + mm(text_feat, dtext_cols, ((0,), (0,)))
    project_part = scatter_rows(
        project_grad.astype(bf16).reshape(blk, channels // blk, 3 * wide_rows)
    ).astype(bf16)

    dmodulated = upstream + row_norm_back(normed_two, inverse_two, dnormed_two)
    dshift = jnp.stack([jnp.sum(dmodulated * after_res, axis=0), jnp.sum(dmodulated, axis=0)])
    dafter = dmodulated * scale_part
    dbranch_own = (keep_own * dafter).astype(bf16)
    dbranch = jnp.concatenate(gather_batch(dbranch_own), axis=0)
    dgrn = mm(dbranch, narrow_weight, ((1,), (1,)))
    sums = jnp.concatenate(
        [per_latent(dgrn * hidden), jnp.sum(dgrn, axis=0, keepdims=True)], axis=0
    )
    sums = sum_over(sums, "blk")
    latent_sums = sums[:batch]
    drelative = gains[0] * latent_sums
    gain_rows = jnp.stack([tree_sum((latent_sums * relative)[d] for d in range(batch)), sums[batch]])
    dmagnitude = drelative / mean_mag - total_over_units(drelative * magnitude) / (
        mean_mag * mean_mag * units
    )
    dhidden = dgrn * spread(gains[0] * relative + 1.0) + hidden * spread(dmagnitude / magnitude)
    slope = gauss + pre_act * jnp.exp(-0.5 * pre_act * pre_act) * 0.3989422804014327
    dpre_wide = keep * dhidden * slope
    dpre = dpre_wide.astype(bf16)
    widen_bias_part = jnp.sum(dpre.astype(f32), axis=0)
    dnormed_one = scatter_batch(split(mm(dpre, wide, ((1,), (1,)))))

    widen_grad = mm(first_in, dpre, ((0,), (0,))).astype(bf16)
    widen_part = scatter_rows(widen_grad.reshape(blk, channels // blk, mine)).astype(bf16)
    narrow_grad = mm(dbranch, second_in, ((0,), (0,))).astype(bf16)
    narrow_sum = scatter_rows(narrow_grad.reshape(blk, channels // blk, mine)).T

    width = mine // ring
    widen_held = jnp.zeros((ring, channels // blk, width), bf16)
    cuts = jnp.stack([widen_part[:, j * width : (j + 1) * width] for j in range(ring)])
    for j in range(ring):
        hops = [
            (b * blk + k, (k // ring) * blk + b * ring + ((k % ring) ^ j))
            for b in range(batch)
            for k in range(blk)
        ]
        piece = lax.ppermute(take(cuts, (ki % ring) ^ j), ("batch", "blk"), hops)
        widen_held = put(widen_held, piece, (ki % ring) ^ j)
    widen_sum = widen_held.reshape(wide_rows, width).astype(f32)

    unit_count = 3 * groups
    out_cols = 3 * channels // blk
    units_of = jnp.stack([project_part[:, u * span : (u + 1) * span] for u in range(unit_count)])
    if out_cols % span == 0 and unit_count * ring == ring * ring * (out_cols // span):
        per_out = out_cols // span
        sources, targets, labels = [], [], []
        for b in range(batch):
            for k in range(blk):
                for unit in range(unit_count):
                    place = (unit % 3) * (channels // span) + b * groups + unit // 3
                    sources.append(b * blk + k)
                    targets.append((k // ring) * blk + place // per_out)
                    labels.append((unit, (k % ring) * per_out + place % per_out))
        me = bi * blk + ki
        project_held = jnp.zeros((ring * per_out, channels // blk, span), bf16)
        for matching in colour(sources, targets, unit_count):
            pick = [0] * (batch * blk)
            drop = [0] * (batch * blk)
            for edge in matching:
                pick[sources[edge]], drop[targets[edge]] = labels[edge][0], labels[edge][1]
            hops = [(sources[edge], targets[edge]) for edge in matching]
            piece = take(units_of, jnp.array(pick, jnp.int32)[me])
            piece = lax.ppermute(piece, ("batch", "blk"), hops)
            project_held = put(project_held, piece, jnp.array(drop, jnp.int32)[me])
        project_sum = jnp.concatenate(
            [
                jnp.concatenate([project_held[r * per_out + p] for p in range(per_out)], axis=1)
                for r in range(ring)
            ],
            axis=0,
        )
    else:
        thirds = jnp.stack(
            [
                jnp.concatenate([units_of[3 * g + third] for g in range(groups)], axis=1)
                for third in range(3)
            ]
        )
        thirds = lax.all_gather(thirds, "batch", axis=2, tiled=True)
        thirds = thirds.reshape(3, channels // blk, channels)
        whole = jnp.concatenate([thirds[third] for third in range(3)], axis=1)
        whole = lax.all_to_all(whole, "blk", split_axis=1, concat_axis=0, tiled=True)
        project_sum = lax.dynamic_slice(whole, (bi * wide_rows, 0), (wide_rows, out_cols))
    project_sum = project_sum.astype(f32)

    dconved = keep_own * row_norm_back(normed_one, inverse_one, dnormed_one)
    grad_ext = halo(dconved.astype(bf16), margin)
    dlatent = dafter
    depth_rows = []
    for tap, (step_row, step_col) in enumerate(taps):
        depth_rows.append(jnp.sum(window(source_ext, step_row, step_col) * dconved, axis=0))
        dlatent = dlatent + window(grad_ext, -step_row, -step_col) * depth_taps[tap]
    latent_grad = dlatent.astype(bf16)

    sums_cols = jnp.sum(dqkv.astype(f32), axis=0) + jnp.sum(dtext_cols.astype(f32), axis=0)
    shift_part = jnp.concatenate(
        [
            sums_cols[g * 3 * span + third * span : g * 3 * span + (third + 1) * span]
            for third in (0, 2)
            for g in range(groups)
        ]
    )
    narrow_units = mine
    pad = max(channels, narrow_units, 2 * wide_rows)

    def line(cells):
        return jnp.pad(cells, (0, pad - cells.shape[0]))

    late = jnp.stack(
        [line(dshift[0]), line(dshift[1])]
        + [
            line(cells)
            for cells in [
                jnp.sum(upstream, axis=0),
                jnp.sum(dbranch_own.astype(f32), axis=0),
                jnp.sum(dconved, axis=0),
            ]
            + depth_rows
            + [shift_part, widen_bias_part]
        ]
    )
    late = sum_over(late, "blk")
    late = jnp.concatenate([late, jnp.stack([line(gain_rows[0]), line(gain_rows[1])])], axis=0)
    members = gather_batch(late)
    both = tree_sum(members)
    output_bias_sum = both[2, :channels]
    narrow_bias_sum = both[3, :channels]
    depth_bias_sum = both[4, :channels]
    depth_weight_sum = both[5:14, :channels]
    outer = [
        jnp.concatenate(
            [
                times[d][:, None] * members[d][0, None, :channels],
                times[d][:, None] * members[d][1, None, :channels],
            ],
            axis=1,
        )
        for d in range(batch)
    ]
    time_weight_sum = tree_sum(outer)
    time_bias_sum = tree_sum(
        jnp.concatenate([members[d][0, :channels], members[d][1, :channels]])
        for d in range(batch)
    )
    ordered = jnp.stack([take(jnp.stack(members), l ^ bi) for l in range(batch)])
    project_bias_sum = jnp.concatenate(
        [
            ordered[:, 14, :wide_rows].reshape(-1),
            ordered[:, 14, wide_rows : 2 * wide_rows].reshape(-1),
        ]
    )
    widen_bias_sum = ordered[:, 15, :mine].reshape(-1)
    gain_sum = jnp.stack([ordered[:, 16, :mine].reshape(-1), ordered[:, 17, :mine].reshape(-1)])

    return (
        block_output[None],
        latent_grad[None],
        depth_weight_sum,
        depth_bias_sum,
        widen_sum,
        widen_bias_sum,
        gain_sum,
        narrow_sum,
        narrow_bias_sum,
        time_weight_sum,
        time_bias_sum,
        text_sum_grad,
        text_bias_sum,
        project_sum,
        project_bias_sum,
        output_sum,
        output_bias_sum,
    )


def solution(mesh):
    rows = P("batch", "blk", None)
    first = P("batch", None)
    both = P("batch", "blk")
    everywhere = P()
    placed = (
        rows,
        first,
        P("batch", None, None),
        first,
        everywhere,
        everywhere,
        first,
        everywhere,
        everywhere,
        first,
        everywhere,
        everywhere,
        everywhere,
        first,
        everywhere,
        first,
        everywhere,
        first,
        everywhere,
        rows,
    )
    given = (
        rows,
        rows,
        everywhere,
        everywhere,
        both,
        everywhere,
        everywhere,
        both,
        everywhere,
        everywhere,
        everywhere,
        both,
        everywhere,
        both,
        everywhere,
        both,
        everywhere,
    )
    return jax.shard_map(
        on_device, mesh=mesh, in_specs=placed, out_specs=given, check_vma=False
    )
```

```python
import jax
import jax.numpy as jnp
from jax import lax
from jax.sharding import PartitionSpec as P

HEADS = 24
HDIM = 64
WIDE = 112

norm_eps = 1e-06
masked_score = -1e30
f32 = jnp.float32
bf16 = jnp.bfloat16


def mm(left, right, dims):
    return lax.dot_general(left, right, (dims, ((), ())), preferred_element_type=f32)


def swap(cells, axis, distance):
    count = lax.axis_size(axis)
    return lax.ppermute(cells, axis, [(i, i ^ distance) for i in range(count)])


def bits_of(count):
    return [1 << n for n in range(count.bit_length() - 1)]


def batch_pair(cells):
    if lax.axis_size("batch") == 4:
        return jnp.stack([cells, swap(cells, "batch", 2)])
    return cells[None]


def batch_all(pair):
    count = lax.axis_size("batch")
    if count == 4:
        mate = swap(pair, "batch", 1)
        return jnp.concatenate([pair[0], mate[0], pair[1], mate[1]], axis=0)
    return jnp.concatenate(
        [pair[0]] + [swap(pair[0], "batch", d) for d in range(1, count)], axis=0
    )


def gather_batch(cells):
    return batch_all(batch_pair(cells))


def gate(*arrays):
    return lax.optimization_barrier(arrays)


def scatter_batch(parts, sent=None, held=()):
    if len(parts) == 4:
        mate = swap(jnp.stack([parts[1], parts[3]]).astype(bf16), "batch", 1)
        far = (parts[2] + mate[1].astype(f32)).astype(bf16)
        if sent is not None:
            sent.extend(gate(far, *held))
            far = sent[0]
        return parts[0] + mate[0].astype(f32) + swap(far, "batch", 2).astype(f32)
    if sent is not None:
        sent.extend(gate(parts[0], *held))
    held = dict(enumerate(parts))
    for bit in bits_of(len(parts)):
        held = {
            place: cells + swap(held[place ^ bit].astype(bf16), "batch", bit).astype(f32)
            for place, cells in held.items()
            if not place & bit
        }
    return held[0]


class Relay:
    def __init__(self, piece, distance):
        me = lax.axis_index("batch")
        self.piece, self.distance = piece, distance
        self.side = (lax.axis_index("blk") // distance) % 2
        self.whole = lax.axis_size("batch") == 4
        self.pieces = [piece(me)]
        self.held = []

    def part(self, member):
        cells = self.piece(member)
        rows = cells.shape[0] // 2
        return lax.dynamic_slice_in_dim(cells, self.side * rows, rows, 0)

    def near(self, *then):
        if not self.whole:
            self.pieces = exchange_batch(self.piece)
            return
        me = lax.axis_index("batch")
        self.pieces.append(swap(after(self.piece(me ^ 1), *then), "batch", 1))

    def far(self, *then):
        if self.whole:
            me = lax.axis_index("batch")
            cells = jnp.stack([self.part(me ^ 2), self.part(me ^ 3)])
            self.held = [swap(after(cells, *then), "batch", 2)]

    def hand_on(self, *then):
        if self.whole:
            cells = after(self.held[0], *then)
            self.held = [cells, swap(cells, "blk", self.distance)]

    def gate(self, value):
        value, *self.held = gate(value, *self.held)
        return value

    def finish(self, *then):
        if self.whole:
            cells, other = self.held
            cells = after(cells, *then)
            low = jnp.where(self.side == 0, cells, other)
            high = jnp.where(self.side == 0, other, cells)
            cells = jnp.concatenate([low, high], axis=1)
            self.pieces = self.pieces + [cells[0], swap(cells[1], "batch", 1)]
        return self.pieces


def exchange_batch(piece):
    me, count = lax.axis_index("batch"), lax.axis_size("batch")
    return [piece(me)] + [swap(piece(me ^ d), "batch", d) for d in range(1, count)]


def tree_sum(pieces):
    pieces = list(pieces)
    while len(pieces) > 1:
        pieces = [pieces[i] + pieces[i + 1] for i in range(0, len(pieces), 2)]
    return pieces[0]


def sum_over(cells, axis):
    count = lax.axis_size(axis)
    if axis == "blk" and count == 8:
        cells = cells + swap(cells, axis, 1)
        return tree_sum([cells] + [swap(cells, axis, d) for d in (2, 4, 6)])
    if count <= 4:
        return tree_sum([cells] + [swap(cells, axis, d) for d in range(1, count)])
    for bit in bits_of(count):
        cells = cells + swap(cells, axis, bit)
    return cells


def after(cells, *others):
    return lax.optimization_barrier((cells,) + others)[0]


def choose(pieces, place):
    if len(pieces) == 2:
        return jnp.where(place == 0, pieces[0], pieces[1])
    return lax.dynamic_index_in_dim(jnp.stack(pieces), place, 0, keepdims=False)


def row_norm(field_rows):
    average = jnp.mean(field_rows, axis=-1, keepdims=True)
    centred = field_rows - average
    spread = jnp.mean(centred * centred, axis=-1, keepdims=True)
    inverse = lax.rsqrt(spread + norm_eps)
    return (centred * inverse, inverse)


def row_norm_back(normed, inverse, upstream):
    first_mean = jnp.mean(upstream, axis=-1, keepdims=True)
    second_mean = jnp.mean(upstream * normed, axis=-1, keepdims=True)
    return inverse * (upstream - first_mean - normed * second_mean)


def attend(queries, keys, values, grad_heads, live):
    scores = mm(queries, keys, ((1,), (1,))) * 0.125
    scores = jnp.where(live, scores, masked_score)
    raised = jnp.exp(scores - jnp.max(scores, axis=1, keepdims=True))
    shares = raised / jnp.sum(raised, axis=1, keepdims=True)
    shares_low = shares.astype(bf16)
    attended = mm(shares_low, values, ((1,), (0,)))
    delta = jnp.sum(grad_heads.astype(f32) * attended, axis=1, keepdims=True)
    dshares = mm(grad_heads, values, ((1,), (1,)))
    dscores = (shares * (dshares - delta)).astype(bf16)
    return (
        attended,
        mm(dscores, keys, ((1,), (0,))) * 0.125,
        mm(dscores, queries, ((0,), (0,))) * 0.125,
        mm(shares_low, grad_heads, ((0,), (0,))),
    )


def on_device(
    latent,
    time_embed,
    text_tokens,
    grid_shape,
    depth_weight,
    depth_bias,
    widen_weight,
    widen_bias,
    response_gain,
    narrow_weight,
    narrow_bias,
    time_weight,
    time_bias,
    text_weight,
    text_bias,
    project_weight,
    project_bias,
    output_weight,
    output_bias,
    cotangent,
):
    _, rows, channels = latent.shape
    batch, blk = lax.axis_size("batch"), lax.axis_size("blk")
    bi, ki = lax.axis_index("batch"), lax.axis_index("blk")
    ring = blk // batch
    plane, lane = ki // ring, ki % ring
    units = widen_weight.shape[1]
    mine = units // batch
    wide_rows = channels // batch
    own_heads = HEADS // batch
    per = -(-own_heads // ring)
    span = per * HDIM
    clip_rows = text_weight.shape[0]
    text_count = text_tokens.shape[1]
    half = batch * rows
    grid = [(b, p, l) for b in range(batch) for p in range(batch) for l in range(ring)]

    def spot(b, p, l):
        return b * blk + p * ring + l

    turned = [(spot(b, p, l), spot(p, b, l)) for b, p, l in grid]

    def turn(cells):
        return lax.ppermute(cells, ("batch", "blk"), turned)

    def lanes(cells):
        return [swap(cells[e - 1], "blk", e) for e in range(1, ring)]

    def by_lane(pieces):
        return [choose(pieces, lane ^ e) for e in range(ring)]

    def halo(cells, margin):
        order = [[spot(b, p, l) for b in range(batch) for l in range(ring)] for p in range(batch)]
        up = [(line[i], line[i + 1]) for line in order for i in range(len(line) - 1)]
        before = lax.ppermute(cells[rows - margin :], ("batch", "blk"), up)
        behind = lax.ppermute(cells[:margin], ("batch", "blk"), [(j, i) for i, j in up])
        return jnp.concatenate([before, cells, behind], axis=0)

    def over_planes(shards):
        members = [[p * ring + l for p in range(batch)] for l in range(ring)]
        return lax.psum_scatter(
            shards, "blk", scatter_dimension=0, tiled=False, axis_index_groups=members
        ).astype(f32)

    first_lane = (lane == 0).astype(f32)
    margin = WIDE + 1
    lat = turn(latent[0])
    facts = turn(
        jnp.concatenate(
            [
                grid_shape.astype(f32),
                time_embed.astype(f32),
                jnp.zeros((1, 126 - time_embed.shape[1]), f32),
            ],
            axis=1,
        )
    )
    source_ext = halo(lat, margin)

    def by_member(pieces):
        held = jnp.zeros((batch,) + pieces[0].shape, bf16)
        for d, piece in enumerate(pieces):
            held = lax.dynamic_update_index_in_dim(held, piece, bi ^ d, 0)
        return held.reshape((-1,) + pieces[0].shape[1:])

    def widen_piece(member):
        return lax.dynamic_slice(widen_weight, (0, member * mine), (wide_rows, mine))

    wide_relay = Relay(widen_piece, ring)
    wide_relay.far()
    wide_relay.near()
    source_ext = wide_relay.gate(source_ext)
    wide_relay.hand_on()
    wide_pieces = wide_relay.finish()

    def grouped(cells):
        extra = ring * span - wide_rows
        if extra:
            cells = [jnp.pad(part, ((0, 0), (0, extra))) for part in cells]
        return [
            jnp.concatenate([part[:, g * span : (g + 1) * span] for part in cells], axis=1)
            for g in range(ring)
        ]

    project_given = after(project_weight, lat)

    def project_piece(member):
        pieces = [
            lax.dynamic_slice(
                project_given, (0, third * channels + member * wide_rows), (wide_rows,) * 2
            )
            for third in range(3)
        ]
        return jnp.concatenate(by_lane(grouped(pieces)), axis=1)

    project_relay = Relay(project_piece, ring)
    project_relay.near()
    project_relay.far()

    grid_w = facts[0, 0].astype(jnp.int32)
    grid_h = facts[0, 1].astype(jnp.int32)
    pixels = grid_w * grid_h
    time_own = facts[:, 2 : 2 + time_embed.shape[1]]

    def rows_of(member_batch, member_lane):
        return (member_batch * ring + member_lane) * rows + jnp.arange(rows, dtype=jnp.int32)

    row_index = rows_of(bi, lane)
    row_of = jnp.floor((row_index.astype(f32) + 0.5) / facts[0, 0]).astype(jnp.int32)
    col_of = row_index - row_of * grid_w
    inside = row_index < pixels
    keep_own = inside.astype(f32)[:, None]

    def valid(step_row, step_col):
        return (
            inside
            & (row_of + step_row >= 0)
            & (row_of + step_row < grid_h)
            & (col_of + step_col >= 0)
            & (col_of + step_col < grid_w)
        )[:, None]

    taps = [(tap // 3 - 1, tap % 3 - 1) for tap in range(9)]
    depth_taps = depth_weight.astype(f32)

    def window(ext, step_row, step_col):
        start = margin + step_row * grid_w + step_col
        moved = lax.dynamic_slice_in_dim(ext, start, rows, 0).astype(f32)
        return jnp.where(valid(step_row, step_col), moved, 0.0)

    conved = jnp.zeros((rows, channels), f32)
    for tap, (step_row, step_col) in enumerate(taps):
        conved = conved + window(source_ext, step_row, step_col) * depth_taps[tap]
    conved = jnp.where(inside[:, None], conved + depth_bias.astype(f32), 0.0)
    normed_one, inverse_one = row_norm(conved)
    first_low = normed_one.astype(bf16)
    first_pair = batch_pair(first_low)
    first_in = batch_all(first_pair)
    first_in = project_relay.gate(first_in)
    project_relay.hand_on(first_in)
    (
        widen_bias,
        response_gain,
        narrow_bias,
        time_weight,
        time_bias,
        text_tokens,
        text_bias,
        project_weight,
        project_bias,
        output_weight,
        output_bias,
        _,
    ) = lax.optimization_barrier(
        (
            widen_bias,
            response_gain,
            narrow_bias,
            time_weight,
            time_bias,
            text_tokens,
            text_bias,
            project_weight,
            project_bias,
            output_weight,
            output_bias,
            first_low,
        )
    )

    half_rows = jnp.concatenate([rows_of(bi ^ d, lane) for d in range(batch)])
    keep = (half_rows < pixels).astype(f32)[:, None]
    widen_shift = lax.dynamic_slice(widen_bias, (bi * mine,), (mine,)).astype(f32)
    pre_act = widen_shift
    for d, piece in enumerate(wide_pieces):
        cells = lax.dynamic_slice(first_in, (0, (bi ^ d) * wide_rows), (half, wide_rows))
        pre_act = pre_act + mm(cells, piece, ((1,), (0,)))
    gauss = 0.5 * (1.0 + lax.erf(pre_act * (0.5**0.5)))
    hidden = pre_act * gauss * keep

    def total(cells):
        own = jnp.broadcast_to(jnp.sum(cells, axis=1, keepdims=True), (1, 128))
        return sum_over(own, "batch")[:, :1]

    def lane_sum(cells):
        bit = 1
        while bit < ring:
            cells = cells + swap(cells, "blk", bit)
            bit *= 2
        return cells

    shift_q = lax.dynamic_slice(project_bias, (bi * wide_rows,), (wide_rows,)).astype(f32)
    shift_v = lax.dynamic_slice(project_bias, (channels + bi * wide_rows,), (wide_rows,)).astype(
        f32
    )
    project_shift = jnp.concatenate(
        by_lane(grouped([shift_q[None], jnp.zeros((1, wide_rows), f32), shift_v[None]])), axis=1
    )
    squares = lane_sum(jnp.sum(hidden * hidden, axis=0, keepdims=True))
    magnitude = jnp.sqrt(squares + norm_eps)
    mean_mag = total(magnitude) / units + norm_eps
    mean_mag = project_relay.gate(mean_mag)
    first_sent = [swap(after(first_pair[0], squares), "blk", e) for e in range(1, ring)]
    mean_mag, *first_sent = gate(mean_mag, *first_sent)
    relative = magnitude / mean_mag

    gains = lax.dynamic_slice(response_gain, (0, bi * mine), (2, mine)).astype(f32)
    second_in = (gains[:1] * (hidden * relative) + gains[1:] + hidden).astype(bf16)
    branch_part = mm(second_in, narrow_weight, ((1,), (0,)))
    def split(cells):
        return [cells[d * rows : (d + 1) * rows] for d in range(batch)]

    cot = turn(after(cotangent[0], mean_mag))
    first_rest = []
    if batch == 4:
        first_rest = [swap(after(first_pair[1], second_in), "blk", e) for e in range(1, ring)]
    leaving = []
    branch = scatter_batch(split(branch_part), leaving, [cot])
    cot = leaving[1]
    branch, *first_rest = gate(branch, *first_rest)
    if batch == 4:
        first_sent = [jnp.stack(pair) for pair in zip(first_sent, first_rest)]
    else:
        first_sent = [cells[None] for cells in first_sent]
    branch = branch + narrow_bias.astype(f32)
    after_res = lat.astype(f32) + keep_own * branch
    shift_scale = mm(time_own.astype(bf16), time_weight, ((1,), (0,))) + time_bias.astype(f32)
    scale_part = 1.0 + shift_scale[:, :channels]
    modulated = after_res * scale_part + shift_scale[:, channels:]
    normed_two, inverse_two = row_norm(modulated)
    attn_low = normed_two.astype(bf16)
    attn_pair = batch_pair(attn_low)
    attn_in = batch_all(attn_pair)
    project_pieces = project_relay.finish(mean_mag)
    projected = project_shift
    for d, piece in enumerate(project_pieces):
        cells = lax.dynamic_slice(attn_in, (0, (bi ^ d) * wide_rows), (half, wide_rows))
        projected = projected + mm(cells, piece, ((1,), (0,)))
    projected = projected.astype(bf16)
    project = by_member([after(piece, projected) for piece in project_pieces])
    first_others = [batch_all(after(cells, projected)) for cells in first_sent]

    output_groups = [output_weight[g * span : (g + 1) * span] for g in range(ring)]
    output_groups = [
        jnp.pad(cells, ((0, span - cells.shape[0]), (0, 0))) for cells in output_groups
    ]
    output_own = jnp.concatenate(by_lane(output_groups), axis=0)

    cot_pair = batch_pair(after(cot, projected))
    cot_rows = batch_all(cot_pair)
    grad_heads = mm(cot_rows, output_own, ((1,), (1,))).astype(bf16)

    def cut(cells, width):
        return [cells[:, e * width : (e + 1) * width] for e in range(ring)]

    def to_heads(cells, width):
        pieces = cut(cells, width)
        return jnp.concatenate([pieces[0]] + lanes(pieces[1:]), axis=0)

    shard = channels // blk

    def lane_columns(cells):
        pieces = [
            jnp.concatenate(
                [
                    cells[..., (p * ring + g) * shard : (p * ring + g + 1) * shard]
                    for p in range(batch)
                ],
                axis=-1,
            )
            for g in range(ring)
        ]
        return by_lane(pieces)

    grad_heads = to_heads(grad_heads, span)

    tokens = lax.dynamic_slice(text_tokens[0], (0, plane * clip_rows), (text_count, clip_rows))
    tokens = turn(after(tokens, first_in))
    soft = jax.nn.silu(tokens.astype(f32)).astype(bf16)
    text_sum = mm(after(soft, second_in), text_weight, ((1,), (0,)))
    for bit in bits_of(batch):
        low = text_sum.astype(bf16)
        low = after(low, projected) if bit > 1 else low
        text_sum = low.astype(f32) + swap(low, "batch", bit).astype(f32)
    text_feat = (text_sum + text_bias.astype(f32)).astype(bf16)
    project_own = project[:, : 3 * span]
    text_proj = (mm(text_feat, project_own, ((1,), (0,))) + project_shift[:, : 3 * span]).astype(
        bf16
    )

    projected = to_heads(projected, 3 * span)
    attn_sent = [swap(after(attn_pair, projected), "blk", e) for e in range(1, ring)]

    projected, grad_heads = gate(projected, grad_heads)
    seq = ring * half
    seq_rows = jnp.concatenate(
        [rows_of(bi ^ d, lane ^ e) for e in range(ring) for d in range(batch)]
        + [jnp.full((text_count,), -1, jnp.int32)]
    )
    live = (seq_rows < pixels)[None, :]
    keys = jnp.concatenate([projected[:, span : 2 * span], text_proj[:, span : 2 * span]], axis=0)
    values = jnp.concatenate([projected[:, 2 * span :], text_proj[:, 2 * span :]], axis=0)
    heads = []
    for head in range(per):
        at = slice(head * HDIM, (head + 1) * HDIM)
        heads.append(attend(projected[:, at], keys[:, at], values[:, at], grad_heads[:, at], live))
        if head == per // 2:
            key_cells, *attn_sent = gate(heads[-1][2], *attn_sent)
            heads[-1] = heads[-1][:2] + (key_cells,) + heads[-1][3:]
    attended, dq, dk, dv = (jnp.concatenate(cells, axis=1).astype(bf16) for cells in zip(*heads))
    dqkv_seq = jnp.concatenate([dq, dk[:seq], dv[:seq]], axis=1)
    cot_sent = [
        swap(cells, "blk", e)
        for e, cells in enumerate(lane_columns(after(cot_pair, grad_heads))[1:], 1)
    ]
    dqkv_seq, *cot_sent = gate(dqkv_seq, *cot_sent)
    cot_lanes = [batch_all(after(cells, dqkv_seq)) for cells in cot_sent]
    sent = [dqkv_seq[e * half : (e + 1) * half] for e in range(ring)]
    dq_sent = lanes([cells[:, :span] for cells in sent[1:]])
    then_sent = lanes([cells[:, span:] for cells in sent[1:]])
    dqkv = [sent[0]]
    for first_cells, then_cells in zip(dq_sent, then_sent):
        dqkv = dqkv + [first_cells, then_cells]
    dqkv = jnp.concatenate(dqkv, axis=1)
    attended_sent = lanes([after(attended, dq_sent[0])] * (ring - 1))
    attn_others = [batch_all(after(cells, dqkv)) for cells in attn_sent]
    quarter = half // 4
    seconds = [second_in[n * quarter : (n + 1) * quarter] for n in range(4)]
    leaving = []
    dnormed_part = mm(dqkv, project, ((1,), (1,)))
    dnormed_two = scatter_batch(split(dnormed_part), leaving)
    second_sent = [lanes([after(seconds[0], leaving[0])] * (ring - 1))]
    dtext_low = jnp.concatenate([jnp.zeros((text_count, span), bf16), dk[seq:], dv[seq:]], axis=1)
    attn_all = jnp.concatenate([after(attn_in, *leaving)] + attn_others, axis=0)
    project_grad = mm(attn_all, dqkv_seq, ((0,), (0,))) + mm(text_feat, dtext_low, ((0,), (0,)))
    project_grad = project_grad.astype(bf16)
    dnormed_two = after(dnormed_two, project_grad)
    project_part = over_planes(project_grad.reshape(batch, wide_rows, 3 * span)).astype(bf16)
    dnormed_two, *held = gate(dnormed_two, *attended_sent, *second_sent[0])
    attended_sent, second_sent[0] = held[: ring - 1], held[ring - 1 :]
    second_sent.append(lanes([after(seconds[1], dnormed_two)] * (ring - 1)))
    attended_all = jnp.concatenate([attended] + attended_sent, axis=1)

    upstream = cot.astype(f32)

    dmodulated = upstream + row_norm_back(normed_two, inverse_two, dnormed_two)
    dshift = [jnp.sum(dmodulated * after_res, axis=0), jnp.sum(dmodulated, axis=0)]
    dafter = dmodulated * scale_part
    dbranch_own = (keep_own * dafter).astype(bf16)
    dbranch_pair = batch_pair(dbranch_own)
    dbranch_pair, *second_sent[1] = gate(dbranch_pair, *second_sent[1])
    second_sent.append(lanes([after(seconds[2], dbranch_own)] * (ring - 1)))
    dbranch = batch_all(dbranch_pair)
    dbranch, *second_sent[2] = gate(dbranch, *second_sent[2])
    dgrn = mm(dbranch, narrow_weight, ((1,), (1,)))
    sums = lane_sum(jnp.stack([jnp.sum(dgrn * hidden, axis=0), jnp.sum(dgrn, axis=0)]))
    drelative = gains[:1] * sums[:1]
    gain_rows = jnp.concatenate([sums[:1] * relative, sums[1:]]) * first_lane
    dmagnitude = drelative / mean_mag - total(drelative * magnitude) / (
        mean_mag * mean_mag * units
    )
    dhidden = dgrn * (gains[:1] * relative + 1.0) + hidden * (dmagnitude / magnitude)
    slope = gauss + pre_act * jnp.exp(-0.5 * pre_act * pre_act) * 0.3989422804014327
    attended_own = jnp.concatenate(
        [attended]
        + [
            jnp.concatenate(
                [
                    attended_all[(f ^ e) * half : ((f ^ e) + 1) * half, e * span : (e + 1) * span]
                    for f in range(ring)
                ],
                axis=0,
            )
            for e in range(1, ring)
        ],
        axis=1,
    )
    att_out = scatter_batch(
        split(mm(after(attended_own[:half], dbranch_own), output_own, ((1,), (0,))))
    )
    att_out = after(att_out, sums)
    block_low = (modulated + att_out + output_bias.astype(f32)).astype(bf16)
    dbranch_sent = [
        swap(cells, "blk", e)
        for e, cells in enumerate(lane_columns(after(dbranch_pair, sums))[1:], 1)
    ]
    dpre = (keep * dhidden * slope).astype(bf16)
    widen_bias_part = jnp.sum(dpre.astype(f32), axis=0)
    wide = by_member([after(piece, projected) for piece in wide_pieces])
    dnormed_part = mm(dpre, wide, ((1,), (1,)))
    dtext_part = mm(after(dtext_low, sums), project_own, ((1,), (1,)))
    for axis, count in (("blk", ring), ("batch", batch)):
        for bit in bits_of(count):
            low = dtext_part.astype(bf16)
            dtext_part = low.astype(f32) + swap(low, axis, bit).astype(f32)
    second_sent.append(lanes([after(seconds[3], sums)] * (ring - 1)))
    leaving = []
    dnormed_one = scatter_batch(
        split(dnormed_part), leaving, [dtext_part, *second_sent[3]]
    )
    dtext = leaving[1].astype(bf16)
    second_sent[3] = leaving[2:]
    second_others = [cells for chunk in zip(*second_sent) for cells in chunk]
    text_cut = [
        jnp.concatenate(
            [dtext[:, (p * ring + g) * shard : (p * ring + g + 1) * shard] for p in range(batch)],
            axis=1,
        )
        for g in range(ring)
    ]
    text_grad = mm(choose(text_cut, lane), soft, ((0,), (0,))).astype(bf16)
    text_sum_grad = over_planes(text_grad.reshape(batch, shard, clip_rows))
    dbranch_lanes = [batch_all(after(cells, leaving[0])) for cells in dbranch_sent]
    dbranch_lane = jnp.concatenate(
        [after(lane_columns(dbranch)[0], *leaving)] + dbranch_lanes, axis=0
    )
    second_all = jnp.concatenate([after(second_in, *leaving)] + second_others, axis=0)
    narrow_grad = mm(dbranch_lane, second_all, ((0,), (0,))).astype(bf16)
    project_part = after(project_part, *leaving)
    out_cols = 3 * channels // blk
    blocks = channels // span
    if out_cols == 3 * span and blocks == blk and blocks % 3 == 2:
        own_block = bi * ring + lane
        pieces = [project_part[:, third * span : (third + 1) * span] for third in range(3)]
        project_sum = []
        for place in range(3):
            hops = []
            for p in range(batch):
                for k in range(blk):
                    b, l = divmod((3 * k + place) % blocks, ring)
                    hops.append((spot(b, p, l), p * blk + k))
            third = (2 * (place - own_block + 3 * blocks)) % 3
            piece = jnp.where(
                third == 0, pieces[0], jnp.where(third == 1, pieces[1], pieces[2])
            )
            project_sum.append(lax.ppermute(piece, ("batch", "blk"), hops))
    else:
        whole = lax.all_gather(turn(project_part), "blk", axis=0, tiled=False)
        whole = whole.reshape(batch, ring, wide_rows, 3, span)
        whole = jnp.transpose(whole, (2, 3, 0, 1, 4)).reshape(wide_rows, 3, batch, ring * span)
        whole = whole[..., :wide_rows].reshape(wide_rows, 3 * channels)
        project_sum = lax.dynamic_slice(whole, (0, ki * out_cols), (wide_rows, out_cols))
        project_sum = [project_sum]

    width = mine // ring
    dpre_cuts = [
        lax.dynamic_slice(dpre, (0, (lane ^ e) * width), (half, width)) for e in range(ring)
    ]
    dpre_lane = jnp.concatenate(
        [after(dpre_cuts[0], narrow_grad)] + lanes(dpre_cuts[1:]), axis=0
    )
    first_all = jnp.concatenate([after(first_in, narrow_grad)] + first_others, axis=0)
    widen_grad = mm(first_all, dpre_lane, ((0,), (0,))).astype(bf16)
    widen_grad = widen_grad.reshape(batch, wide_rows, width)
    widen_pieces = exchange_batch(
        lambda member: lax.dynamic_index_in_dim(widen_grad, member, 0, keepdims=False)
    )
    dnormed_one = after(dnormed_one, widen_grad)
    dnormed_one, *project_sum = gate(dnormed_one, *project_sum)
    narrow_sum = over_planes(after(narrow_grad, text_sum_grad).reshape(batch, shard, mine))
    dconved = keep_own * row_norm_back(normed_one, inverse_one, dnormed_one)
    dconved_low, *widen_pieces[3:] = gate(dconved.astype(bf16), *widen_pieces[3:])

    attended_natural = jnp.concatenate(
        by_lane([attended_own[:, e * span : (e + 1) * span] for e in range(ring)]), axis=1
    )[:, :wide_rows]
    cot_lane = jnp.concatenate(
        [after(lane_columns(cot_rows)[0], dbranch_own)] + cot_lanes, axis=0
    )
    output_grad = mm(cot_lane, attended_natural, ((0,), (0,))).astype(bf16)
    output_sum = over_planes(output_grad.reshape(batch, shard, wide_rows))


    grad_ext = halo(dconved_low, margin)
    grad_ext, *widen_pieces[:3] = gate(grad_ext, *widen_pieces[:3])
    text_bias_part = jnp.sum(dtext.astype(f32), axis=0) * (first_lane * (bi == 0).astype(f32))
    block_output = turn(after(block_low, widen_pieces[2]))
    dlatent = dafter
    depth_rows = []
    for tap, (step_row, step_col) in enumerate(taps):
        depth_rows.append(jnp.sum(window(source_ext, step_row, step_col) * dconved, axis=0))
        dlatent = dlatent + window(grad_ext, -step_row, -step_col) * depth_taps[tap]
    latent_grad = turn(dlatent.astype(bf16))
    group_cols = jnp.sum(dqkv_seq.astype(f32), axis=0) + jnp.sum(dtext_low.astype(f32), axis=0)
    shift_part = []
    for third in (0, 2):
        cells = group_cols[third * span : (third + 1) * span]
        cells = [jnp.where(lane == g, cells, jnp.zeros_like(cells)) for g in range(ring)]
        shift_part.append(jnp.concatenate(cells)[:wide_rows])
    pad = max(channels, mine, 2 * wide_rows)

    def line(cells):
        return jnp.pad(cells, (0, pad - cells.shape[0]))

    late = [
        jnp.sum(upstream, axis=0),
        jnp.sum(dbranch_own.astype(f32), axis=0),
        text_bias_part,
        jnp.sum(dconved, axis=0),
    ] + depth_rows
    shared = len(late)
    late = late + [jnp.concatenate(shift_part), widen_bias_part, gain_rows[0], gain_rows[1]]
    sliced = len(late)
    once = first_lane * (bi == 0).astype(f32)
    late = lane_sum(jnp.stack([line(cells) for cells in late + dshift + [time_own[0] * once]]))
    members = gather_batch(late).reshape((batch,) + late.shape)
    both = tree_sum(members)
    late = jnp.concatenate(
        [both[:shared], members[:, shared:sliced].reshape(-1, pad), both[sliced:]]
    )
    by_plane = [late] + [swap(late, "blk", ring * d) for d in range(1, batch)]
    both = tree_sum(by_plane)
    members = both[shared : shared + batch * (sliced - shared)].reshape(batch, -1, pad)
    widen_held = jnp.stack(widen_pieces)

    def for_plane(member):
        return lax.dynamic_index_in_dim(widen_held, member ^ bi, 0, keepdims=False)

    widen_sum = over_planes(
        after(jnp.stack([for_plane(p) for p in range(batch)]), narrow_sum)
    )
    arrived = grad_ext

    output_bias_sum, narrow_bias_sum, text_bias_sum, depth_bias_sum = (
        both[i, :channels] for i in range(4)
    )
    depth_weight_sum = both[4:shared, :channels]
    shifts = [
        jnp.concatenate([by_plane[d][-3, :channels], by_plane[d][-2, :channels]])
        for d in range(batch)
    ]
    time_bias_sum = tree_sum(shifts)
    time_weight_sum = tree_sum(
        by_plane[d][-1, : time_embed.shape[1]][:, None] * shifts[d][None, :]
        for d in range(batch)
    )
    ordered = jnp.stack(
        [lax.dynamic_index_in_dim(members, l ^ bi, 0, keepdims=False) for l in range(batch)]
    )
    project_bias_sum = jnp.concatenate(
        [
            ordered[:, 0, :wide_rows].reshape(-1),
            ordered[:, 0, wide_rows : 2 * wide_rows].reshape(-1),
        ]
    )
    widen_bias_sum = ordered[:, 1, :mine].reshape(-1)
    gain_sum = jnp.stack([ordered[:, 2, :mine].reshape(-1), ordered[:, 3, :mine].reshape(-1)])

    project_sum = jnp.concatenate([after(project_sum[0], arrived)] + project_sum[1:], axis=1)
    project_sum = project_sum.astype(f32)

    return (
        block_output[None],
        latent_grad[None],
        depth_weight_sum,
        depth_bias_sum,
        widen_sum,
        widen_bias_sum,
        gain_sum,
        after(narrow_sum, arrived).T,
        narrow_bias_sum,
        time_weight_sum,
        time_bias_sum,
        after(text_sum_grad, arrived).T,
        text_bias_sum,
        project_sum,
        project_bias_sum,
        after(output_sum, arrived).T,
        output_bias_sum,
    )


def solution(mesh):
    rows = P("batch", "blk", None)
    first = P("batch", None)
    both = P("batch", "blk")
    everywhere = P()
    placed = (
        rows,
        first,
        P("batch", None, None),
        first,
        everywhere,
        everywhere,
        first,
        everywhere,
        everywhere,
        first,
        everywhere,
        everywhere,
        everywhere,
        first,
        everywhere,
        first,
        everywhere,
        first,
        everywhere,
        rows,
    )
    given = (
        rows,
        rows,
        everywhere,
        everywhere,
        both,
        everywhere,
        everywhere,
        both,
        everywhere,
        everywhere,
        everywhere,
        both,
        everywhere,
        both,
        everywhere,
        both,
        everywhere,
    )
    return jax.shard_map(
        on_device, mesh=mesh, in_specs=placed, out_specs=given, check_vma=False
    )
```

```python
import jax
import jax.numpy as jnp
from jax import lax
from jax.sharding import PartitionSpec as P

HEADS = 24
HDIM = 64
WIDE = 112

norm_eps = 1e-06
masked_score = -1e30
f32 = jnp.float32
bf16 = jnp.bfloat16


def mm(left, right, dims):
    return lax.dot_general(left, right, (dims, ((), ())), preferred_element_type=f32)


def swap(cells, axis, distance):
    count = lax.axis_size(axis)
    return lax.ppermute(cells, axis, [(i, i ^ distance) for i in range(count)])


def bits_of(count):
    return [1 << n for n in range(count.bit_length() - 1)]


def batch_pair(cells):
    if lax.axis_size("batch") == 4:
        return jnp.stack([cells, swap(cells, "batch", 2)])
    return cells[None]


def batch_all(pair):
    count = lax.axis_size("batch")
    if count == 4:
        mate = swap(pair, "batch", 1)
        return jnp.concatenate([pair[0], mate[0], pair[1], mate[1]], axis=0)
    return jnp.concatenate(
        [pair[0]] + [swap(pair[0], "batch", d) for d in range(1, count)], axis=0
    )


def gather_batch(cells):
    return batch_all(batch_pair(cells))


def gate(*arrays):
    return lax.optimization_barrier(arrays)


def scatter_batch(parts, sent=None, held=()):
    if len(parts) == 4:
        mate = swap(jnp.stack([parts[1], parts[3]]).astype(bf16), "batch", 1)
        far = (parts[2] + mate[1].astype(f32)).astype(bf16)
        if sent is not None:
            sent.extend(gate(far, *held))
            far = sent[0]
        return parts[0] + mate[0].astype(f32) + swap(far, "batch", 2).astype(f32)
    if sent is not None:
        sent.extend(gate(parts[0], *held))
    held = dict(enumerate(parts))
    for bit in bits_of(len(parts)):
        held = {
            place: cells + swap(held[place ^ bit].astype(bf16), "batch", bit).astype(f32)
            for place, cells in held.items()
            if not place & bit
        }
    return held[0]


class Relay:
    def __init__(self, piece, distance):
        me = lax.axis_index("batch")
        self.piece, self.distance = piece, distance
        self.side = (lax.axis_index("blk") // distance) % 2
        self.whole = lax.axis_size("batch") == 4
        self.pieces = [piece(me)]
        self.held = []

    def part(self, member):
        cells = self.piece(member)
        rows = cells.shape[0] // 2
        return lax.dynamic_slice_in_dim(cells, self.side * rows, rows, 0)

    def near(self, *then):
        if not self.whole:
            self.pieces = exchange_batch(self.piece)
            return
        me = lax.axis_index("batch")
        self.pieces.append(swap(after(self.piece(me ^ 1), *then), "batch", 1))

    def far(self, *then):
        if self.whole:
            me = lax.axis_index("batch")
            cells = jnp.stack([self.part(me ^ 2), self.part(me ^ 3)])
            self.held = [swap(after(cells, *then), "batch", 2)]

    def hand_on(self, *then):
        if self.whole:
            cells = after(self.held[0], *then)
            self.held = [cells, swap(cells, "blk", self.distance)]

    def gate(self, value):
        value, *self.held = gate(value, *self.held)
        return value

    def finish(self, *then):
        if self.whole:
            cells, other = self.held
            cells = after(cells, *then)
            low = jnp.where(self.side == 0, cells, other)
            high = jnp.where(self.side == 0, other, cells)
            cells = jnp.concatenate([low, high], axis=1)
            self.pieces = self.pieces + [cells[0], swap(cells[1], "batch", 1)]
        return self.pieces


def exchange_batch(piece):
    me, count = lax.axis_index("batch"), lax.axis_size("batch")
    return [piece(me)] + [swap(piece(me ^ d), "batch", d) for d in range(1, count)]


def tree_sum(pieces):
    pieces = list(pieces)
    while len(pieces) > 1:
        pieces = [pieces[i] + pieces[i + 1] for i in range(0, len(pieces), 2)]
    return pieces[0]


def sum_over(cells, axis):
    count = lax.axis_size(axis)
    if axis == "blk" and count == 8:
        cells = cells + swap(cells, axis, 1)
        return tree_sum([cells] + [swap(cells, axis, d) for d in (2, 4, 6)])
    if count <= 4:
        return tree_sum([cells] + [swap(cells, axis, d) for d in range(1, count)])
    for bit in bits_of(count):
        cells = cells + swap(cells, axis, bit)
    return cells


def after(cells, *others):
    return lax.optimization_barrier((cells,) + others)[0]


def choose(pieces, place):
    if len(pieces) == 2:
        return jnp.where(place == 0, pieces[0], pieces[1])
    return lax.dynamic_index_in_dim(jnp.stack(pieces), place, 0, keepdims=False)


def row_norm(field_rows):
    average = jnp.mean(field_rows, axis=-1, keepdims=True)
    centred = field_rows - average
    spread = jnp.mean(centred * centred, axis=-1, keepdims=True)
    inverse = lax.rsqrt(spread + norm_eps)
    return (centred * inverse, inverse)


def row_norm_back(normed, inverse, upstream):
    first_mean = jnp.mean(upstream, axis=-1, keepdims=True)
    second_mean = jnp.mean(upstream * normed, axis=-1, keepdims=True)
    return inverse * (upstream - first_mean - normed * second_mean)


def attend(queries, keys, values, grad_heads, live):
    scores = mm(queries, keys, ((1,), (1,))) * 0.125
    scores = jnp.where(live, scores, masked_score)
    raised = jnp.exp(scores - jnp.max(scores, axis=1, keepdims=True))
    shares = raised / jnp.sum(raised, axis=1, keepdims=True)
    shares_low = shares.astype(bf16)
    attended = mm(shares_low, values, ((1,), (0,)))
    delta = jnp.sum(grad_heads.astype(f32) * attended, axis=1, keepdims=True)
    dshares = mm(grad_heads, values, ((1,), (1,)))
    dscores = (shares * (dshares - delta)).astype(bf16)
    return (
        attended,
        mm(dscores, keys, ((1,), (0,))) * 0.125,
        mm(dscores, queries, ((0,), (0,))) * 0.125,
        mm(shares_low, grad_heads, ((0,), (0,))),
    )


def on_device(
    latent,
    time_embed,
    text_tokens,
    grid_shape,
    depth_weight,
    depth_bias,
    widen_weight,
    widen_bias,
    response_gain,
    narrow_weight,
    narrow_bias,
    time_weight,
    time_bias,
    text_weight,
    text_bias,
    project_weight,
    project_bias,
    output_weight,
    output_bias,
    cotangent,
):
    _, rows, channels = latent.shape
    batch, blk = lax.axis_size("batch"), lax.axis_size("blk")
    bi, ki = lax.axis_index("batch"), lax.axis_index("blk")
    ring = blk // batch
    plane, lane = ki // ring, ki % ring
    units = widen_weight.shape[1]
    mine = units // batch
    wide_rows = channels // batch
    own_heads = HEADS // batch
    per = -(-own_heads // ring)
    span = per * HDIM
    clip_rows = text_weight.shape[0]
    text_count = text_tokens.shape[1]
    half = batch * rows
    grid = [(b, p, l) for b in range(batch) for p in range(batch) for l in range(ring)]

    def spot(b, p, l):
        return b * blk + p * ring + l

    turned = [(spot(b, p, l), spot(p, b, l)) for b, p, l in grid]

    def turn(cells):
        return lax.ppermute(cells, ("batch", "blk"), turned)

    def lanes(cells):
        return [swap(cells[e - 1], "blk", e) for e in range(1, ring)]

    def by_lane(pieces):
        return [choose(pieces, lane ^ e) for e in range(ring)]

    def halo(cells, margin):
        order = [[spot(b, p, l) for b in range(batch) for l in range(ring)] for p in range(batch)]
        up = [(line[i], line[i + 1]) for line in order for i in range(len(line) - 1)]
        before = lax.ppermute(cells[rows - margin :], ("batch", "blk"), up)
        behind = lax.ppermute(cells[:margin], ("batch", "blk"), [(j, i) for i, j in up])
        return jnp.concatenate([before, cells, behind], axis=0)

    def over_planes(shards):
        members = [[p * ring + l for p in range(batch)] for l in range(ring)]
        return lax.psum_scatter(
            shards, "blk", scatter_dimension=0, tiled=False, axis_index_groups=members
        ).astype(f32)

    first_lane = (lane == 0).astype(f32)
    def plane_pieces(shards):
        if batch != 4:
            return [over_planes(shards)]
        own = [lax.dynamic_index_in_dim(shards, plane ^ d, 0, keepdims=False) for d in range(4)]
        return own[:1] + [swap(own[d], "blk", ring * d) for d in range(1, 4)]

    def add_up(pieces):
        return tree_sum([cells.astype(f32) for cells in pieces])

    margin = WIDE + 1
    lat = turn(latent[0])
    facts = turn(
        jnp.concatenate(
            [
                grid_shape.astype(f32),
                time_embed.astype(f32),
                jnp.zeros((1, 126 - time_embed.shape[1]), f32),
            ],
            axis=1,
        )
    )
    source_ext = halo(lat, margin)

    def by_member(pieces):
        held = jnp.zeros((batch,) + pieces[0].shape, bf16)
        for d, piece in enumerate(pieces):
            held = lax.dynamic_update_index_in_dim(held, piece, bi ^ d, 0)
        return held.reshape((-1,) + pieces[0].shape[1:])

    def widen_piece(member):
        return lax.dynamic_slice(widen_weight, (0, member * mine), (wide_rows, mine))

    wide_relay = Relay(widen_piece, ring)
    wide_relay.far()
    wide_relay.near()
    source_ext = wide_relay.gate(source_ext)
    wide_relay.hand_on()
    wide_pieces = wide_relay.finish()

    def grouped(cells):
        extra = ring * span - wide_rows
        if extra:
            cells = [jnp.pad(part, ((0, 0), (0, extra))) for part in cells]
        return [
            jnp.concatenate([part[:, g * span : (g + 1) * span] for part in cells], axis=1)
            for g in range(ring)
        ]

    project_given = after(project_weight, lat)

    def project_piece(member):
        pieces = [
            lax.dynamic_slice(
                project_given, (0, third * channels + member * wide_rows), (wide_rows,) * 2
            )
            for third in range(3)
        ]
        return jnp.concatenate(by_lane(grouped(pieces)), axis=1)

    project_relay = Relay(project_piece, ring)
    project_relay.near()
    project_relay.far()

    grid_w = facts[0, 0].astype(jnp.int32)
    grid_h = facts[0, 1].astype(jnp.int32)
    pixels = grid_w * grid_h
    time_own = facts[:, 2 : 2 + time_embed.shape[1]]

    def rows_of(member_batch, member_lane):
        return (member_batch * ring + member_lane) * rows + jnp.arange(rows, dtype=jnp.int32)

    row_index = rows_of(bi, lane)
    row_of = jnp.floor((row_index.astype(f32) + 0.5) / facts[0, 0]).astype(jnp.int32)
    col_of = row_index - row_of * grid_w
    inside = row_index < pixels
    keep_own = inside.astype(f32)[:, None]

    def valid(step_row, step_col):
        return (
            inside
            & (row_of + step_row >= 0)
            & (row_of + step_row < grid_h)
            & (col_of + step_col >= 0)
            & (col_of + step_col < grid_w)
        )[:, None]

    taps = [(tap // 3 - 1, tap % 3 - 1) for tap in range(9)]
    depth_taps = depth_weight.astype(f32)

    def window(ext, step_row, step_col):
        start = margin + step_row * grid_w + step_col
        moved = lax.dynamic_slice_in_dim(ext, start, rows, 0).astype(f32)
        return jnp.where(valid(step_row, step_col), moved, 0.0)

    conved = jnp.zeros((rows, channels), f32)
    for tap, (step_row, step_col) in enumerate(taps):
        conved = conved + window(source_ext, step_row, step_col) * depth_taps[tap]
    conved = jnp.where(inside[:, None], conved + depth_bias.astype(f32), 0.0)
    normed_one, inverse_one = row_norm(conved)
    first_low = normed_one.astype(bf16)
    first_pair = batch_pair(first_low)
    first_in = batch_all(first_pair)
    first_in = project_relay.gate(first_in)
    project_relay.hand_on(first_in)
    (
        widen_bias,
        response_gain,
        narrow_bias,
        time_weight,
        time_bias,
        text_tokens,
        text_bias,
        project_weight,
        project_bias,
        output_weight,
        output_bias,
        _,
    ) = lax.optimization_barrier(
        (
            widen_bias,
            response_gain,
            narrow_bias,
            time_weight,
            time_bias,
            text_tokens,
            text_bias,
            project_weight,
            project_bias,
            output_weight,
            output_bias,
            first_low,
        )
    )

    half_rows = jnp.concatenate([rows_of(bi ^ d, lane) for d in range(batch)])
    keep = (half_rows < pixels).astype(f32)[:, None]
    widen_shift = lax.dynamic_slice(widen_bias, (bi * mine,), (mine,)).astype(f32)
    pre_act = widen_shift
    for d, piece in enumerate(wide_pieces):
        cells = lax.dynamic_slice(first_in, (0, (bi ^ d) * wide_rows), (half, wide_rows))
        pre_act = pre_act + mm(cells, piece, ((1,), (0,)))
    gauss = 0.5 * (1.0 + lax.erf(pre_act * (0.5**0.5)))
    hidden = pre_act * gauss * keep

    def total(cells):
        own = jnp.broadcast_to(jnp.sum(cells, axis=1, keepdims=True), (1, 128))
        return sum_over(own, "batch")[:, :1]

    def lane_sum(cells):
        bit = 1
        while bit < ring:
            cells = cells + swap(cells, "blk", bit)
            bit *= 2
        return cells

    shift_q = lax.dynamic_slice(project_bias, (bi * wide_rows,), (wide_rows,)).astype(f32)
    shift_v = lax.dynamic_slice(project_bias, (channels + bi * wide_rows,), (wide_rows,)).astype(
        f32
    )
    project_shift = jnp.concatenate(
        by_lane(grouped([shift_q[None], jnp.zeros((1, wide_rows), f32), shift_v[None]])), axis=1
    )
    squares = lane_sum(jnp.sum(hidden * hidden, axis=0, keepdims=True))
    magnitude = jnp.sqrt(squares + norm_eps)
    mean_mag = total(magnitude) / units + norm_eps
    mean_mag = project_relay.gate(mean_mag)
    first_sent = [swap(after(first_pair[0], squares), "blk", e) for e in range(1, ring)]
    mean_mag, *first_sent = gate(mean_mag, *first_sent)
    relative = magnitude / mean_mag

    gains = lax.dynamic_slice(response_gain, (0, bi * mine), (2, mine)).astype(f32)
    second_in = (gains[:1] * (hidden * relative) + gains[1:] + hidden).astype(bf16)
    branch_part = mm(second_in, narrow_weight, ((1,), (0,)))
    def split(cells):
        return [cells[d * rows : (d + 1) * rows] for d in range(batch)]

    cot = turn(after(cotangent[0], mean_mag))
    first_rest = []
    if batch == 4:
        first_rest = [swap(after(first_pair[1], second_in), "blk", e) for e in range(1, ring)]
    leaving = []
    branch = scatter_batch(split(branch_part), leaving, [cot])
    cot = leaving[1]
    branch, *first_rest = gate(branch, *first_rest)
    if batch == 4:
        first_sent = [jnp.stack(pair) for pair in zip(first_sent, first_rest)]
    else:
        first_sent = [cells[None] for cells in first_sent]
    branch = branch + narrow_bias.astype(f32)
    after_res = lat.astype(f32) + keep_own * branch
    shift_scale = mm(time_own.astype(bf16), time_weight, ((1,), (0,))) + time_bias.astype(f32)
    scale_part = 1.0 + shift_scale[:, :channels]
    modulated = after_res * scale_part + shift_scale[:, channels:]
    normed_two, inverse_two = row_norm(modulated)
    attn_low = normed_two.astype(bf16)
    attn_pair = batch_pair(attn_low)
    attn_in = batch_all(attn_pair)
    project_pieces = project_relay.finish(mean_mag)
    projected = project_shift
    for d, piece in enumerate(project_pieces):
        cells = lax.dynamic_slice(attn_in, (0, (bi ^ d) * wide_rows), (half, wide_rows))
        projected = projected + mm(cells, piece, ((1,), (0,)))
    projected = projected.astype(bf16)
    project = by_member([after(piece, projected) for piece in project_pieces])
    first_others = [batch_all(after(cells, projected)) for cells in first_sent]

    output_groups = [output_weight[g * span : (g + 1) * span] for g in range(ring)]
    output_groups = [
        jnp.pad(cells, ((0, span - cells.shape[0]), (0, 0))) for cells in output_groups
    ]
    output_own = jnp.concatenate(by_lane(output_groups), axis=0)

    cot_pair = batch_pair(after(cot, projected))
    cot_rows = batch_all(cot_pair)
    grad_heads = mm(cot_rows, output_own, ((1,), (1,))).astype(bf16)

    def cut(cells, width):
        return [cells[:, e * width : (e + 1) * width] for e in range(ring)]

    def to_heads(cells, width):
        pieces = cut(cells, width)
        return jnp.concatenate([pieces[0]] + lanes(pieces[1:]), axis=0)

    shard = channels // blk

    def lane_columns(cells):
        pieces = [
            jnp.concatenate(
                [
                    cells[..., (p * ring + g) * shard : (p * ring + g + 1) * shard]
                    for p in range(batch)
                ],
                axis=-1,
            )
            for g in range(ring)
        ]
        return by_lane(pieces)

    grad_heads = to_heads(grad_heads, span)

    tokens = lax.dynamic_slice(text_tokens[0], (0, plane * clip_rows), (text_count, clip_rows))
    tokens = turn(after(tokens, first_in))
    soft = jax.nn.silu(tokens.astype(f32)).astype(bf16)
    text_sum = mm(after(soft, second_in), text_weight, ((1,), (0,)))
    for bit in bits_of(batch):
        low = text_sum.astype(bf16)
        low = after(low, projected) if bit > 1 else low
        text_sum = low.astype(f32) + swap(low, "batch", bit).astype(f32)
    text_feat = (text_sum + text_bias.astype(f32)).astype(bf16)
    project_own = project[:, : 3 * span]
    text_proj = (mm(text_feat, project_own, ((1,), (0,))) + project_shift[:, : 3 * span]).astype(
        bf16
    )

    projected = to_heads(projected, 3 * span)

    wide = by_member([after(piece, attn_in) for piece in wide_pieces])
    projected, grad_heads, project, wide = gate(projected, grad_heads, project, wide)
    seq = ring * half
    seq_rows = jnp.concatenate(
        [rows_of(bi ^ d, lane ^ e) for e in range(ring) for d in range(batch)]
        + [jnp.full((text_count,), -1, jnp.int32)]
    )
    live = (seq_rows < pixels)[None, :]
    keys = jnp.concatenate([projected[:, span : 2 * span], text_proj[:, span : 2 * span]], axis=0)
    values = jnp.concatenate([projected[:, 2 * span :], text_proj[:, 2 * span :]], axis=0)
    heads = []
    for head in range(per):
        at = slice(head * HDIM, (head + 1) * HDIM)
        heads.append(attend(projected[:, at], keys[:, at], values[:, at], grad_heads[:, at], live))
    attended, dq, dk, dv = (jnp.concatenate(cells, axis=1).astype(bf16) for cells in zip(*heads))
    dqkv_seq = jnp.concatenate([dq, dk[:seq], dv[:seq]], axis=1)
    cot_sent = [
        swap(cells, "blk", e)
        for e, cells in enumerate(lane_columns(after(cot_pair, grad_heads))[1:], 1)
    ]
    dqkv_seq, *cot_sent = gate(dqkv_seq, *cot_sent)
    cot_lanes = [batch_all(after(cells, dqkv_seq)) for cells in cot_sent]
    sent = [dqkv_seq[e * half : (e + 1) * half] for e in range(ring)]
    dq_sent = lanes([cells[:, :span] for cells in sent[1:]])
    then_sent = lanes([cells[:, span:] for cells in sent[1:]])
    dqkv = [sent[0]]
    for first_cells, then_cells in zip(dq_sent, then_sent):
        dqkv = dqkv + [first_cells, then_cells]
    dqkv = jnp.concatenate(dqkv, axis=1)
    attended_sent = lanes([after(attended, dq_sent[0])] * (ring - 1))
    attn_sent = [swap(after(attn_pair, dq_sent[0]), "blk", e) for e in range(1, ring)]
    quarter = half // 4
    seconds = [second_in[n * quarter : (n + 1) * quarter] for n in range(4)]
    leaving = []
    dnormed_part = mm(dqkv, project, ((1,), (1,)))
    dnormed_two = scatter_batch(split(dnormed_part), leaving)
    second_sent = [lanes([after(seconds[0], leaving[0])] * (ring - 1))]
    dtext_low = jnp.concatenate([jnp.zeros((text_count, span), bf16), dk[seq:], dv[seq:]], axis=1)
    second_sent = [lanes([after(seconds[0], leaving[0])] * (ring - 1))]
    dtext_low = jnp.concatenate([jnp.zeros((text_count, span), bf16), dk[seq:], dv[seq:]], axis=1)
    second_sent.append(lanes([after(seconds[1], dnormed_two)] * (ring - 1)))
    attended_all = jnp.concatenate([attended] + attended_sent, axis=1)

    upstream = cot.astype(f32)

    dmodulated = upstream + row_norm_back(normed_two, inverse_two, dnormed_two)
    dshift = [jnp.sum(dmodulated * after_res, axis=0), jnp.sum(dmodulated, axis=0)]
    dafter = dmodulated * scale_part
    dbranch_own = (keep_own * dafter).astype(bf16)
    dbranch_pair = batch_pair(dbranch_own)
    dbranch_pair, *second_sent[0] = gate(dbranch_pair, *second_sent[0])
    attn_others = [batch_all(after(cells, dbranch_own)) for cells in attn_sent]
    attn_all = jnp.concatenate([after(attn_in, dbranch_own)] + attn_others, axis=0)
    project_grad = mm(attn_all, dqkv_seq, ((0,), (0,))) + mm(text_feat, dtext_low, ((0,), (0,)))
    project_grad = project_grad.astype(bf16)
    project_part = over_planes(project_grad.reshape(batch, wide_rows, 3 * span)).astype(bf16)
    dbranch = after(batch_all(dbranch_pair), project_grad)
    dbranch, *second_sent[1] = gate(dbranch, *second_sent[1])
    attended_own = jnp.concatenate(
        [attended]
        + [
            jnp.concatenate(
                [
                    attended_all[(f ^ e) * half : ((f ^ e) + 1) * half, e * span : (e + 1) * span]
                    for f in range(ring)
                ],
                axis=0,
            )
            for e in range(1, ring)
        ],
        axis=1,
    )
    attended_natural = jnp.concatenate(
        by_lane([attended_own[:, e * span : (e + 1) * span] for e in range(ring)]), axis=1
    )[:, :wide_rows]
    cot_lane = jnp.concatenate(
        [after(lane_columns(cot_rows)[0], dqkv)] + cot_lanes, axis=0
    )
    output_grad = mm(cot_lane, attended_natural, ((0,), (0,))).astype(bf16)
    output_pieces = plane_pieces(output_grad.reshape(batch, shard, wide_rows))
    dbranch, *output_pieces = gate(dbranch, *output_pieces)
    dgrn = mm(dbranch, narrow_weight, ((1,), (1,)))
    sums = lane_sum(jnp.stack([jnp.sum(dgrn * hidden, axis=0), jnp.sum(dgrn, axis=0)]))
    att_out = scatter_batch(
        split(mm(after(attended_own[:half], dbranch_own), output_own, ((1,), (0,))))
    )
    sums, att_out = gate(sums, att_out)
    drelative = gains[:1] * sums[:1]
    gain_rows = jnp.concatenate([sums[:1] * relative, sums[1:]]) * first_lane
    dmagnitude = drelative / mean_mag - total(drelative * magnitude) / (
        mean_mag * mean_mag * units
    )
    dhidden = dgrn * (gains[:1] * relative + 1.0) + hidden * (dmagnitude / magnitude)
    slope = gauss + pre_act * jnp.exp(-0.5 * pre_act * pre_act) * 0.3989422804014327
    att_out = after(att_out, dmagnitude)
    block_low = (modulated + att_out + output_bias.astype(f32)).astype(bf16)
    dbranch_sent = [
        swap(cells, "blk", e)
        for e, cells in enumerate(lane_columns(after(dbranch_pair, sums))[1:], 1)
    ]
    dpre = (keep * dhidden * slope).astype(bf16)
    widen_bias_part = jnp.sum(dpre.astype(f32), axis=0)
    dnormed_part = mm(dpre, wide, ((1,), (1,)))
    second_sent.append(lanes([after(seconds[2], sums)] * (ring - 1)))
    second_sent.append(lanes([after(seconds[3], sums)] * (ring - 1)))
    dtext_part = mm(after(dtext_low, sums), project_own, ((1,), (1,)))
    for bit in bits_of(ring):
        low = dtext_part.astype(bf16)
        dtext_part = low.astype(f32) + swap(low, "blk", bit).astype(f32)
    leaving = []
    dnormed_one = scatter_batch(split(dnormed_part), leaving)
    project_part = after(project_part, leaving[0])
    out_cols = 3 * channels // blk
    blocks = channels // span
    if out_cols == 3 * span and blocks == blk and blocks % 3 == 2:
        own_block = bi * ring + lane
        pieces = [project_part[:, third * span : (third + 1) * span] for third in range(3)]
        project_sum = []
        for place in range(3):
            hops = []
            for p in range(batch):
                for k in range(blk):
                    b, l = divmod((3 * k + place) % blocks, ring)
                    hops.append((spot(b, p, l), p * blk + k))
            third = (2 * (place - own_block + 3 * blocks)) % 3
            piece = jnp.where(
                third == 0, pieces[0], jnp.where(third == 1, pieces[1], pieces[2])
            )
            project_sum.append(lax.ppermute(piece, ("batch", "blk"), hops))
    else:
        whole = lax.all_gather(turn(project_part), "blk", axis=0, tiled=False)
        whole = whole.reshape(batch, ring, wide_rows, 3, span)
        whole = jnp.transpose(whole, (2, 3, 0, 1, 4)).reshape(wide_rows, 3, batch, ring * span)
        whole = whole[..., :wide_rows].reshape(wide_rows, 3 * channels)
        project_sum = lax.dynamic_slice(whole, (0, ki * out_cols), (wide_rows, out_cols))
        project_sum = [project_sum]

    width = mine // ring
    dpre_cuts = [
        lax.dynamic_slice(dpre, (0, (lane ^ e) * width), (half, width)) for e in range(ring)
    ]
    dpre_sent = lanes(dpre_cuts[1:])
    block_output = turn(after(block_low, leaving[0]))
    waiting = [project_sum, block_output, dbranch_sent, second_sent[2], second_sent[3], dpre_sent]
    dnormed_one, waiting = lax.optimization_barrier((dnormed_one, waiting))
    project_sum, block_output, dbranch_sent, second_sent[2], second_sent[3], dpre_sent = waiting
    second_others = [cells for chunk in zip(*second_sent) for cells in chunk]
    dbranch_lanes = [batch_all(after(cells, dnormed_one)) for cells in dbranch_sent]
    dbranch_lane = jnp.concatenate(
        [after(lane_columns(dbranch)[0], dnormed_one)] + dbranch_lanes, axis=0
    )
    second_all = jnp.concatenate([after(second_in, dnormed_one)] + second_others, axis=0)
    narrow_grad = mm(dbranch_lane, second_all, ((0,), (0,))).astype(bf16)
    dpre_lane = jnp.concatenate(
        [after(dpre_cuts[0], narrow_grad)] + dpre_sent, axis=0
    )
    first_all = jnp.concatenate([after(first_in, narrow_grad)] + first_others, axis=0)
    widen_grad = mm(first_all, dpre_lane, ((0,), (0,))).astype(bf16)
    widen_grad = widen_grad.reshape(batch, wide_rows, width)
    widen_pieces = exchange_batch(
        lambda member: lax.dynamic_index_in_dim(widen_grad, member, 0, keepdims=False)
    )
    for bit in bits_of(batch):
        low = dtext_part.astype(bf16)
        low = after(low, leaving[0] if bit == 1 else narrow_grad)
        dtext_part = low.astype(f32) + swap(low, "batch", bit).astype(f32)
    dtext = dtext_part.astype(bf16)
    narrow_sum = over_planes(after(narrow_grad, project_part).reshape(batch, shard, mine))
    dconved = keep_own * row_norm_back(normed_one, inverse_one, after(dnormed_one, narrow_grad))
    dconved_low = dconved.astype(bf16)

    grad_ext = halo(dconved_low, margin)
    text_cut = [
        jnp.concatenate(
            [dtext[:, (p * ring + g) * shard : (p * ring + g + 1) * shard] for p in range(batch)],
            axis=1,
        )
        for g in range(ring)
    ]
    text_grad = mm(choose(text_cut, lane), soft, ((0,), (0,))).astype(bf16)
    text_pieces = plane_pieces(text_grad.reshape(batch, shard, clip_rows))
    text_bias_part = jnp.sum(dtext.astype(f32), axis=0) * (first_lane * (bi == 0).astype(f32))
    dlatent = dafter
    depth_rows = []
    for tap, (step_row, step_col) in enumerate(taps):
        depth_rows.append(jnp.sum(window(source_ext, step_row, step_col) * dconved, axis=0))
        dlatent = dlatent + window(grad_ext, -step_row, -step_col) * depth_taps[tap]
    latent_grad = turn(dlatent.astype(bf16))
    group_cols = jnp.sum(dqkv_seq.astype(f32), axis=0) + jnp.sum(dtext_low.astype(f32), axis=0)
    shift_part = []
    for third in (0, 2):
        cells = group_cols[third * span : (third + 1) * span]
        cells = [jnp.where(lane == g, cells, jnp.zeros_like(cells)) for g in range(ring)]
        shift_part.append(jnp.concatenate(cells)[:wide_rows])
    pad = max(channels, mine, 2 * wide_rows)

    def line(cells):
        return jnp.pad(cells, (0, pad - cells.shape[0]))

    late = [
        jnp.sum(upstream, axis=0),
        jnp.sum(dbranch_own.astype(f32), axis=0),
        text_bias_part,
        jnp.sum(dconved, axis=0),
    ] + depth_rows
    shared = len(late)
    late = late + [jnp.concatenate(shift_part), widen_bias_part, gain_rows[0], gain_rows[1]]
    sliced = len(late)
    once = first_lane * (bi == 0).astype(f32)
    late = lane_sum(jnp.stack([line(cells) for cells in late + dshift + [time_own[0] * once]]))
    late, *widen_pieces = gate(late, *widen_pieces)
    by_plane = [late] + [swap(late, "blk", ring * d) for d in range(1, batch)]
    by_plane[0], *text_pieces = gate(by_plane[0], *text_pieces)
    late = jnp.concatenate(
        [tree_sum([cells[:sliced] for cells in by_plane])] + [cells[sliced:] for cells in by_plane]
    )
    members = gather_batch(late).reshape((batch,) + late.shape)
    both = tree_sum(members)
    widen_held = after(
        jnp.stack(widen_pieces), narrow_sum, by_plane[0]
    )

    def for_plane(member):
        return lax.dynamic_index_in_dim(widen_held, member ^ bi, 0, keepdims=False)

    widen_sum = over_planes(jnp.stack([for_plane(p) for p in range(batch)]))
    arrived = grad_ext

    output_bias_sum, narrow_bias_sum, text_bias_sum, depth_bias_sum = (
        both[i, :channels] for i in range(4)
    )
    depth_weight_sum = both[4:shared, :channels]
    shifts = [
        jnp.concatenate([both[sliced + 3 * d, :channels], both[sliced + 3 * d + 1, :channels]])
        for d in range(batch)
    ]
    time_bias_sum = tree_sum(shifts)
    time_weight_sum = tree_sum(
        both[sliced + 3 * d + 2, : time_embed.shape[1]][:, None] * shifts[d][None, :]
        for d in range(batch)
    )
    ordered = jnp.stack(
        [lax.dynamic_index_in_dim(members[:, shared:sliced], l ^ bi, 0, keepdims=False) for l in range(batch)]
    )
    project_bias_sum = jnp.concatenate(
        [
            ordered[:, 0, :wide_rows].reshape(-1),
            ordered[:, 0, wide_rows : 2 * wide_rows].reshape(-1),
        ]
    )
    widen_bias_sum = ordered[:, 1, :mine].reshape(-1)
    gain_sum = jnp.stack([ordered[:, 2, :mine].reshape(-1), ordered[:, 3, :mine].reshape(-1)])

    project_sum = jnp.concatenate([after(project_sum[0], arrived)] + project_sum[1:], axis=1)
    project_sum = project_sum.astype(f32)

    return (
        block_output[None],
        latent_grad[None],
        depth_weight_sum,
        depth_bias_sum,
        widen_sum,
        widen_bias_sum,
        gain_sum,
        after(narrow_sum, arrived).T,
        narrow_bias_sum,
        time_weight_sum,
        time_bias_sum,
        add_up(text_pieces).T,
        text_bias_sum,
        project_sum,
        project_bias_sum,
        after(add_up(output_pieces), arrived).T,
        output_bias_sum,
    )


def solution(mesh):
    rows = P("batch", "blk", None)
    first = P("batch", None)
    both = P("batch", "blk")
    everywhere = P()
    placed = (
        rows,
        first,
        P("batch", None, None),
        first,
        everywhere,
        everywhere,
        first,
        everywhere,
        everywhere,
        first,
        everywhere,
        everywhere,
        everywhere,
        first,
        everywhere,
        first,
        everywhere,
        first,
        everywhere,
        rows,
    )
    given = (
        rows,
        rows,
        everywhere,
        everywhere,
        both,
        everywhere,
        everywhere,
        both,
        everywhere,
        everywhere,
        everywhere,
        both,
        everywhere,
        both,
        everywhere,
        both,
        everywhere,
    )
    return jax.shard_map(
        on_device, mesh=mesh, in_specs=placed, out_specs=given, check_vma=False
    )
```

```python
import jax
import jax.numpy as jnp
from jax import lax
from jax.sharding import PartitionSpec as P

HEADS = 24
HDIM = 64
WIDE = 112

norm_eps = 1e-06
masked_score = -1e30
f32 = jnp.float32
bf16 = jnp.bfloat16


def mm(left, right, dims):
    return lax.dot_general(left, right, (dims, ((), ())), preferred_element_type=f32)


def swap(cells, axis, distance):
    count = lax.axis_size(axis)
    return lax.ppermute(cells, axis, [(i, i ^ distance) for i in range(count)])


def bits_of(count):
    return [1 << n for n in range(count.bit_length() - 1)]


def batch_pair(cells):
    if lax.axis_size("batch") == 4:
        return jnp.stack([cells, swap(cells, "batch", 2)])
    return cells[None]


def batch_all(pair):
    count = lax.axis_size("batch")
    if count == 4:
        mate = swap(pair, "batch", 1)
        return jnp.concatenate([pair[0], mate[0], pair[1], mate[1]], axis=0)
    return jnp.concatenate(
        [pair[0]] + [swap(pair[0], "batch", d) for d in range(1, count)], axis=0
    )


def gather_batch(cells):
    return batch_all(batch_pair(cells))


def gate(*arrays):
    return lax.optimization_barrier(arrays)


def scatter_batch(parts, sent=None, held=()):
    if len(parts) == 4:
        mate = swap(jnp.stack([parts[1], parts[3]]).astype(bf16), "batch", 1)
        far = (parts[2] + mate[1].astype(f32)).astype(bf16)
        if sent is not None:
            sent.extend(gate(far, *held))
            far = sent[0]
        return parts[0] + mate[0].astype(f32) + swap(far, "batch", 2).astype(f32)
    if sent is not None:
        sent.extend(gate(parts[0], *held))
    held = dict(enumerate(parts))
    for bit in bits_of(len(parts)):
        held = {
            place: cells + swap(held[place ^ bit].astype(bf16), "batch", bit).astype(f32)
            for place, cells in held.items()
            if not place & bit
        }
    return held[0]


class Relay:
    def __init__(self, piece, distance):
        me = lax.axis_index("batch")
        self.piece, self.distance = piece, distance
        self.side = (lax.axis_index("blk") // distance) % 2
        self.whole = lax.axis_size("batch") == 4
        self.pieces = [piece(me)]
        self.held = []

    def part(self, member):
        cells = self.piece(member)
        rows = cells.shape[0] // 2
        return lax.dynamic_slice_in_dim(cells, self.side * rows, rows, 0)

    def near(self, *then):
        if not self.whole:
            self.pieces = exchange_batch(self.piece)
            return
        me = lax.axis_index("batch")
        self.pieces.append(swap(after(self.piece(me ^ 1), *then), "batch", 1))

    def far(self, *then):
        if self.whole:
            me = lax.axis_index("batch")
            cells = jnp.stack([self.part(me ^ 2), self.part(me ^ 3)])
            self.held = [swap(after(cells, *then), "batch", 2)]

    def hand_on(self, *then):
        if self.whole:
            cells = after(self.held[0], *then)
            self.held = [cells, swap(cells, "blk", self.distance)]

    def gate(self, value):
        value, *self.held = gate(value, *self.held)
        return value

    def finish(self, *then):
        if self.whole:
            cells, other = self.held
            cells = after(cells, *then)
            low = jnp.where(self.side == 0, cells, other)
            high = jnp.where(self.side == 0, other, cells)
            cells = jnp.concatenate([low, high], axis=1)
            self.pieces = self.pieces + [cells[0], swap(cells[1], "batch", 1)]
        return self.pieces


def exchange_batch(piece):
    me, count = lax.axis_index("batch"), lax.axis_size("batch")
    return [piece(me)] + [swap(piece(me ^ d), "batch", d) for d in range(1, count)]


def tree_sum(pieces):
    pieces = list(pieces)
    while len(pieces) > 1:
        pieces = [pieces[i] + pieces[i + 1] for i in range(0, len(pieces), 2)]
    return pieces[0]


def sum_over(cells, axis):
    count = lax.axis_size(axis)
    if axis == "blk" and count == 8:
        cells = cells + swap(cells, axis, 1)
        return tree_sum([cells] + [swap(cells, axis, d) for d in (2, 4, 6)])
    if count <= 4:
        return tree_sum([cells] + [swap(cells, axis, d) for d in range(1, count)])
    for bit in bits_of(count):
        cells = cells + swap(cells, axis, bit)
    return cells


def after(cells, *others):
    return lax.optimization_barrier((cells,) + others)[0]


def choose(pieces, place):
    if len(pieces) == 2:
        return jnp.where(place == 0, pieces[0], pieces[1])
    return lax.dynamic_index_in_dim(jnp.stack(pieces), place, 0, keepdims=False)


def row_norm(field_rows):
    average = jnp.mean(field_rows, axis=-1, keepdims=True)
    centred = field_rows - average
    spread = jnp.mean(centred * centred, axis=-1, keepdims=True)
    inverse = lax.rsqrt(spread + norm_eps)
    return (centred * inverse, inverse)


def row_norm_back(normed, inverse, upstream):
    first_mean = jnp.mean(upstream, axis=-1, keepdims=True)
    second_mean = jnp.mean(upstream * normed, axis=-1, keepdims=True)
    return inverse * (upstream - first_mean - normed * second_mean)


def attend(queries, keys, values, grad_heads, live):
    scores = mm(queries, keys, ((1,), (1,))) * 0.125
    scores = jnp.where(live, scores, masked_score)
    raised = jnp.exp(scores - jnp.max(scores, axis=1, keepdims=True))
    shares = raised / jnp.sum(raised, axis=1, keepdims=True)
    shares_low = shares.astype(bf16)
    attended = mm(shares_low, values, ((1,), (0,)))
    delta = jnp.sum(grad_heads.astype(f32) * attended, axis=1, keepdims=True)
    dshares = mm(grad_heads, values, ((1,), (1,)))
    dscores = (shares * (dshares - delta)).astype(bf16)
    return (
        attended,
        mm(dscores, keys, ((1,), (0,))) * 0.125,
        mm(dscores, queries, ((0,), (0,))) * 0.125,
        mm(shares_low, grad_heads, ((0,), (0,))),
    )


def on_device(
    latent,
    time_embed,
    text_tokens,
    grid_shape,
    depth_weight,
    depth_bias,
    widen_weight,
    widen_bias,
    response_gain,
    narrow_weight,
    narrow_bias,
    time_weight,
    time_bias,
    text_weight,
    text_bias,
    project_weight,
    project_bias,
    output_weight,
    output_bias,
    cotangent,
):
    _, rows, channels = latent.shape
    batch, blk = lax.axis_size("batch"), lax.axis_size("blk")
    bi, ki = lax.axis_index("batch"), lax.axis_index("blk")
    ring = blk // batch
    plane, lane = ki // ring, ki % ring
    units = widen_weight.shape[1]
    mine = units // batch
    wide_rows = channels // batch
    own_heads = HEADS // batch
    per = -(-own_heads // ring)
    span = per * HDIM
    clip_rows = text_weight.shape[0]
    text_count = text_tokens.shape[1]
    half = batch * rows
    grid = [(b, p, l) for b in range(batch) for p in range(batch) for l in range(ring)]

    def spot(b, p, l):
        return b * blk + p * ring + l

    turned = [(spot(b, p, l), spot(p, b, l)) for b, p, l in grid]

    def turn(cells):
        return lax.ppermute(cells, ("batch", "blk"), turned)

    def lanes(cells):
        return [swap(cells[e - 1], "blk", e) for e in range(1, ring)]

    def by_lane(pieces):
        return [choose(pieces, lane ^ e) for e in range(ring)]

    def halo(cells, margin):
        order = [[spot(b, p, l) for b in range(batch) for l in range(ring)] for p in range(batch)]
        up = [(line[i], line[i + 1]) for line in order for i in range(len(line) - 1)]
        before = lax.ppermute(cells[rows - margin :], ("batch", "blk"), up)
        behind = lax.ppermute(cells[:margin], ("batch", "blk"), [(j, i) for i, j in up])
        return jnp.concatenate([before, cells, behind], axis=0)

    def over_planes(shards):
        members = [[p * ring + l for p in range(batch)] for l in range(ring)]
        return lax.psum_scatter(
            shards, "blk", scatter_dimension=0, tiled=False, axis_index_groups=members
        ).astype(f32)

    first_lane = (lane == 0).astype(f32)
    def plane_pieces(shards):
        if batch != 4:
            return [over_planes(shards)]
        own = [lax.dynamic_index_in_dim(shards, plane ^ d, 0, keepdims=False) for d in range(4)]
        return own[:1] + [swap(own[d], "blk", ring * d) for d in range(1, 4)]

    def add_up(pieces):
        return tree_sum([cells.astype(f32) for cells in pieces])

    margin = WIDE + 1
    lat = turn(latent[0])
    facts = turn(
        jnp.concatenate(
            [
                grid_shape.astype(f32),
                time_embed.astype(f32),
                jnp.zeros((1, 126 - time_embed.shape[1]), f32),
            ],
            axis=1,
        )
    )
    source_ext = halo(lat, margin)

    def by_member(pieces):
        held = jnp.zeros((batch,) + pieces[0].shape, bf16)
        for d, piece in enumerate(pieces):
            held = lax.dynamic_update_index_in_dim(held, piece, bi ^ d, 0)
        return held.reshape((-1,) + pieces[0].shape[1:])

    def widen_piece(member):
        return lax.dynamic_slice(widen_weight, (0, member * mine), (wide_rows, mine))

    wide_relay = Relay(widen_piece, ring)
    wide_relay.far()
    wide_relay.near()
    source_ext = wide_relay.gate(source_ext)
    wide_relay.hand_on()
    wide_pieces = wide_relay.finish()

    def grouped(cells):
        extra = ring * span - wide_rows
        if extra:
            cells = [jnp.pad(part, ((0, 0), (0, extra))) for part in cells]
        return [
            jnp.concatenate([part[:, g * span : (g + 1) * span] for part in cells], axis=1)
            for g in range(ring)
        ]

    project_given = after(project_weight, lat)

    def project_piece(member):
        pieces = [
            lax.dynamic_slice(
                project_given, (0, third * channels + member * wide_rows), (wide_rows,) * 2
            )
            for third in range(3)
        ]
        return jnp.concatenate(by_lane(grouped(pieces)), axis=1)

    project_relay = Relay(project_piece, ring)
    project_relay.near()
    project_relay.far()

    grid_w = facts[0, 0].astype(jnp.int32)
    grid_h = facts[0, 1].astype(jnp.int32)
    pixels = grid_w * grid_h
    time_own = facts[:, 2 : 2 + time_embed.shape[1]]

    def rows_of(member_batch, member_lane):
        return (member_batch * ring + member_lane) * rows + jnp.arange(rows, dtype=jnp.int32)

    row_index = rows_of(bi, lane)
    row_of = jnp.floor((row_index.astype(f32) + 0.5) / facts[0, 0]).astype(jnp.int32)
    col_of = row_index - row_of * grid_w
    inside = row_index < pixels
    keep_own = inside.astype(f32)[:, None]

    def valid(step_row, step_col):
        return (
            inside
            & (row_of + step_row >= 0)
            & (row_of + step_row < grid_h)
            & (col_of + step_col >= 0)
            & (col_of + step_col < grid_w)
        )[:, None]

    taps = [(tap // 3 - 1, tap % 3 - 1) for tap in range(9)]
    depth_taps = depth_weight.astype(f32)

    def window(ext, step_row, step_col):
        start = margin + step_row * grid_w + step_col
        moved = lax.dynamic_slice_in_dim(ext, start, rows, 0).astype(f32)
        return jnp.where(valid(step_row, step_col), moved, 0.0)

    conved = jnp.zeros((rows, channels), f32)
    for tap, (step_row, step_col) in enumerate(taps):
        conved = conved + window(source_ext, step_row, step_col) * depth_taps[tap]
    conved = jnp.where(inside[:, None], conved + depth_bias.astype(f32), 0.0)
    normed_one, inverse_one = row_norm(conved)
    first_low = normed_one.astype(bf16)
    first_pair = batch_pair(first_low)
    first_in = batch_all(first_pair)
    first_in = project_relay.gate(first_in)
    project_relay.hand_on(first_in)
    (
        widen_bias,
        response_gain,
        narrow_bias,
        time_weight,
        time_bias,
        text_tokens,
        text_bias,
        project_weight,
        project_bias,
        output_weight,
        output_bias,
        _,
    ) = lax.optimization_barrier(
        (
            widen_bias,
            response_gain,
            narrow_bias,
            time_weight,
            time_bias,
            text_tokens,
            text_bias,
            project_weight,
            project_bias,
            output_weight,
            output_bias,
            first_low,
        )
    )

    half_rows = jnp.concatenate([rows_of(bi ^ d, lane) for d in range(batch)])
    keep = (half_rows < pixels).astype(f32)[:, None]
    widen_shift = lax.dynamic_slice(widen_bias, (bi * mine,), (mine,)).astype(f32)
    pre_act = widen_shift
    for d, piece in enumerate(wide_pieces):
        cells = lax.dynamic_slice(first_in, (0, (bi ^ d) * wide_rows), (half, wide_rows))
        pre_act = pre_act + mm(cells, piece, ((1,), (0,)))
    gauss = 0.5 * (1.0 + lax.erf(pre_act * (0.5**0.5)))
    hidden = pre_act * gauss * keep

    def total(cells):
        own = jnp.broadcast_to(jnp.sum(cells, axis=1, keepdims=True), (1, 128))
        return sum_over(own, "batch")[:, :1]

    def lane_sum(cells):
        bit = 1
        while bit < ring:
            cells = cells + swap(cells, "blk", bit)
            bit *= 2
        return cells

    shift_q = lax.dynamic_slice(project_bias, (bi * wide_rows,), (wide_rows,)).astype(f32)
    shift_v = lax.dynamic_slice(project_bias, (channels + bi * wide_rows,), (wide_rows,)).astype(
        f32
    )
    project_shift = jnp.concatenate(
        by_lane(grouped([shift_q[None], jnp.zeros((1, wide_rows), f32), shift_v[None]])), axis=1
    )
    squares = lane_sum(jnp.sum(hidden * hidden, axis=0, keepdims=True))
    magnitude = jnp.sqrt(squares + norm_eps)
    mean_mag = total(magnitude) / units + norm_eps
    mean_mag = project_relay.gate(mean_mag)
    first_sent = [swap(after(first_pair[0], squares), "blk", e) for e in range(1, ring)]
    mean_mag, *first_sent = gate(mean_mag, *first_sent)
    relative = magnitude / mean_mag

    gains = lax.dynamic_slice(response_gain, (0, bi * mine), (2, mine)).astype(f32)
    second_in = (gains[:1] * (hidden * relative) + gains[1:] + hidden).astype(bf16)
    branch_part = mm(second_in, narrow_weight, ((1,), (0,)))
    def split(cells):
        return [cells[d * rows : (d + 1) * rows] for d in range(batch)]

    cot = turn(after(cotangent[0], mean_mag))
    first_rest = []
    if batch == 4:
        first_rest = [swap(after(first_pair[1], second_in), "blk", e) for e in range(1, ring)]
    leaving = []
    branch = scatter_batch(split(branch_part), leaving, [cot])
    cot = leaving[1]
    branch, *first_rest = gate(branch, *first_rest)
    if batch == 4:
        first_sent = [jnp.stack(pair) for pair in zip(first_sent, first_rest)]
    else:
        first_sent = [cells[None] for cells in first_sent]
    branch = branch + narrow_bias.astype(f32)
    after_res = lat.astype(f32) + keep_own * branch
    shift_scale = mm(time_own.astype(bf16), time_weight, ((1,), (0,))) + time_bias.astype(f32)
    scale_part = 1.0 + shift_scale[:, :channels]
    modulated = after_res * scale_part + shift_scale[:, channels:]
    normed_two, inverse_two = row_norm(modulated)
    attn_low = normed_two.astype(bf16)
    attn_pair = batch_pair(attn_low)
    attn_in = batch_all(attn_pair)
    project_pieces = project_relay.finish(mean_mag)
    projected = project_shift
    for d, piece in enumerate(project_pieces):
        cells = lax.dynamic_slice(attn_in, (0, (bi ^ d) * wide_rows), (half, wide_rows))
        projected = projected + mm(cells, piece, ((1,), (0,)))
    projected = projected.astype(bf16)
    project = by_member([after(piece, projected) for piece in project_pieces])
    first_others = [batch_all(after(cells, projected)) for cells in first_sent]

    output_groups = [output_weight[g * span : (g + 1) * span] for g in range(ring)]
    output_groups = [
        jnp.pad(cells, ((0, span - cells.shape[0]), (0, 0))) for cells in output_groups
    ]
    output_own = jnp.concatenate(by_lane(output_groups), axis=0)

    cot_pair = batch_pair(after(cot, projected))
    cot_rows = batch_all(cot_pair)
    grad_heads = mm(cot_rows, output_own, ((1,), (1,))).astype(bf16)

    def cut(cells, width):
        return [cells[:, e * width : (e + 1) * width] for e in range(ring)]

    def to_heads(cells, width):
        pieces = cut(cells, width)
        return jnp.concatenate([pieces[0]] + lanes(pieces[1:]), axis=0)

    shard = channels // blk

    def lane_columns(cells):
        pieces = [
            jnp.concatenate(
                [
                    cells[..., (p * ring + g) * shard : (p * ring + g + 1) * shard]
                    for p in range(batch)
                ],
                axis=-1,
            )
            for g in range(ring)
        ]
        return by_lane(pieces)

    grad_heads = to_heads(grad_heads, span)

    tokens = lax.dynamic_slice(text_tokens[0], (0, plane * clip_rows), (text_count, clip_rows))
    tokens = turn(after(tokens, first_in))
    soft = jax.nn.silu(tokens.astype(f32)).astype(bf16)
    text_sum = mm(after(soft, second_in), text_weight, ((1,), (0,)))
    for bit in bits_of(batch):
        low = text_sum.astype(bf16)
        low = after(low, projected) if bit > 1 else low
        text_sum = low.astype(f32) + swap(low, "batch", bit).astype(f32)
    text_feat = (text_sum + text_bias.astype(f32)).astype(bf16)
    project_own = project[:, : 3 * span]
    text_proj = (mm(text_feat, project_own, ((1,), (0,))) + project_shift[:, : 3 * span]).astype(
        bf16
    )

    projected = to_heads(projected, 3 * span)

    wide = by_member([after(piece, attn_in) for piece in wide_pieces])
    projected, grad_heads, project, wide = gate(projected, grad_heads, project, wide)
    seq = ring * half
    seq_rows = jnp.concatenate(
        [rows_of(bi ^ d, lane ^ e) for e in range(ring) for d in range(batch)]
        + [jnp.full((text_count,), -1, jnp.int32)]
    )
    live = (seq_rows < pixels)[None, :]
    keys = jnp.concatenate([projected[:, span : 2 * span], text_proj[:, span : 2 * span]], axis=0)
    values = jnp.concatenate([projected[:, 2 * span :], text_proj[:, 2 * span :]], axis=0)
    heads = []
    for head in range(per):
        at = slice(head * HDIM, (head + 1) * HDIM)
        heads.append(attend(projected[:, at], keys[:, at], values[:, at], grad_heads[:, at], live))
    attended, dq, dk, dv = (jnp.concatenate(cells, axis=1).astype(bf16) for cells in zip(*heads))
    dqkv_seq = jnp.concatenate([dq, dk[:seq], dv[:seq]], axis=1)
    cot_sent = [
        swap(cells, "blk", e)
        for e, cells in enumerate(lane_columns(after(cot_pair, grad_heads))[1:], 1)
    ]
    dqkv_seq, *cot_sent = gate(dqkv_seq, *cot_sent)
    cot_lanes = [batch_all(after(cells, dqkv_seq)) for cells in cot_sent]
    sent = [dqkv_seq[e * half : (e + 1) * half] for e in range(ring)]
    dq_sent = lanes([cells[:, :span] for cells in sent[1:]])
    then_sent = lanes([cells[:, span:] for cells in sent[1:]])
    dqkv = [sent[0]]
    for first_cells, then_cells in zip(dq_sent, then_sent):
        dqkv = dqkv + [first_cells, then_cells]
    dqkv = jnp.concatenate(dqkv, axis=1)
    attended_sent = lanes([after(attended, dq_sent[0])] * (ring - 1))
    attn_sent = [swap(after(attn_pair, dq_sent[0]), "blk", e) for e in range(1, ring)]
    quarter = half // 4
    seconds = [second_in[n * quarter : (n + 1) * quarter] for n in range(4)]
    leaving = []
    dnormed_part = mm(dqkv, project, ((1,), (1,)))
    dnormed_two = scatter_batch(split(dnormed_part), leaving)
    second_sent = [lanes([after(seconds[0], leaving[0])] * (ring - 1))]
    dtext_low = jnp.concatenate([jnp.zeros((text_count, span), bf16), dk[seq:], dv[seq:]], axis=1)
    second_sent = [lanes([after(seconds[0], leaving[0])] * (ring - 1))]
    dtext_low = jnp.concatenate([jnp.zeros((text_count, span), bf16), dk[seq:], dv[seq:]], axis=1)
    second_sent.append(lanes([after(seconds[1], dnormed_two)] * (ring - 1)))
    attended_all = jnp.concatenate([attended] + attended_sent, axis=1)

    upstream = cot.astype(f32)

    dmodulated = upstream + row_norm_back(normed_two, inverse_two, dnormed_two)
    dshift = [jnp.sum(dmodulated * after_res, axis=0), jnp.sum(dmodulated, axis=0)]
    dafter = dmodulated * scale_part
    dbranch_own = (keep_own * dafter).astype(bf16)
    dbranch_pair = batch_pair(dbranch_own)
    dbranch_pair, *second_sent[0] = gate(dbranch_pair, *second_sent[0])
    attn_others = [batch_all(after(cells, dbranch_own)) for cells in attn_sent]
    attn_all = jnp.concatenate([after(attn_in, dbranch_own)] + attn_others, axis=0)
    project_grad = mm(attn_all, dqkv_seq, ((0,), (0,))) + mm(text_feat, dtext_low, ((0,), (0,)))
    project_grad = project_grad.astype(bf16)
    project_part = over_planes(project_grad.reshape(batch, wide_rows, 3 * span)).astype(bf16)
    dbranch = after(batch_all(dbranch_pair), project_grad)
    dbranch, *second_sent[1] = gate(dbranch, *second_sent[1])
    attended_own = jnp.concatenate(
        [attended]
        + [
            jnp.concatenate(
                [
                    attended_all[(f ^ e) * half : ((f ^ e) + 1) * half, e * span : (e + 1) * span]
                    for f in range(ring)
                ],
                axis=0,
            )
            for e in range(1, ring)
        ],
        axis=1,
    )
    attended_natural = jnp.concatenate(
        by_lane([attended_own[:, e * span : (e + 1) * span] for e in range(ring)]), axis=1
    )[:, :wide_rows]
    cot_lane = jnp.concatenate(
        [after(lane_columns(cot_rows)[0], dqkv)] + cot_lanes, axis=0
    )
    output_grad = mm(cot_lane, attended_natural, ((0,), (0,))).astype(bf16)
    output_grad = after(output_grad, dbranch_own)
    output_pieces = plane_pieces(output_grad.reshape(batch, shard, wide_rows))
    dbranch, *output_pieces = gate(dbranch, *output_pieces)
    dgrn = mm(dbranch, narrow_weight, ((1,), (1,)))
    sums = lane_sum(jnp.stack([jnp.sum(dgrn * hidden, axis=0), jnp.sum(dgrn, axis=0)]))
    att_out = scatter_batch(
        split(mm(after(attended_own[:half], dbranch_own), output_own, ((1,), (0,))))
    )
    sums, att_out = gate(sums, att_out)
    drelative = gains[:1] * sums[:1]
    gain_rows = jnp.concatenate([sums[:1] * relative, sums[1:]]) * first_lane
    dmagnitude = drelative / mean_mag - total(drelative * magnitude) / (
        mean_mag * mean_mag * units
    )
    dhidden = dgrn * (gains[:1] * relative + 1.0) + hidden * (dmagnitude / magnitude)
    slope = gauss + pre_act * jnp.exp(-0.5 * pre_act * pre_act) * 0.3989422804014327
    att_out = after(att_out, dmagnitude)
    block_low = (modulated + att_out + output_bias.astype(f32)).astype(bf16)
    dbranch_sent = [
        swap(cells, "blk", e)
        for e, cells in enumerate(lane_columns(after(dbranch_pair, sums))[1:], 1)
    ]
    dpre = (keep * dhidden * slope).astype(bf16)
    widen_bias_part = jnp.sum(dpre.astype(f32), axis=0)
    dnormed_part = mm(dpre, wide, ((1,), (1,)))
    second_sent.append(lanes([after(seconds[2], sums)] * (ring - 1)))
    second_sent.append(lanes([after(seconds[3], sums)] * (ring - 1)))
    dtext_part = mm(after(dtext_low, sums), project_own, ((1,), (1,)))
    for bit in bits_of(ring):
        low = dtext_part.astype(bf16)
        dtext_part = low.astype(f32) + swap(low, "blk", bit).astype(f32)
    leaving = []
    dnormed_one = scatter_batch(split(dnormed_part), leaving)
    project_part = after(project_part, leaving[0])
    out_cols = 3 * channels // blk
    blocks = channels // span
    if out_cols == 3 * span and blocks == blk and blocks % 3 == 2:
        own_block = bi * ring + lane
        pieces = [project_part[:, third * span : (third + 1) * span] for third in range(3)]
        project_sum = []
        for place in range(3):
            hops = []
            for p in range(batch):
                for k in range(blk):
                    b, l = divmod((3 * k + place) % blocks, ring)
                    hops.append((spot(b, p, l), p * blk + k))
            third = (2 * (place - own_block + 3 * blocks)) % 3
            piece = jnp.where(
                third == 0, pieces[0], jnp.where(third == 1, pieces[1], pieces[2])
            )
            project_sum.append(lax.ppermute(piece, ("batch", "blk"), hops))
    else:
        whole = lax.all_gather(turn(project_part), "blk", axis=0, tiled=False)
        whole = whole.reshape(batch, ring, wide_rows, 3, span)
        whole = jnp.transpose(whole, (2, 3, 0, 1, 4)).reshape(wide_rows, 3, batch, ring * span)
        whole = whole[..., :wide_rows].reshape(wide_rows, 3 * channels)
        project_sum = lax.dynamic_slice(whole, (0, ki * out_cols), (wide_rows, out_cols))
        project_sum = [project_sum]

    width = mine // ring
    dpre_cuts = [
        lax.dynamic_slice(dpre, (0, (lane ^ e) * width), (half, width)) for e in range(ring)
    ]
    dpre_sent = lanes(dpre_cuts[1:])
    block_output = turn(after(block_low, leaving[0]))
    dbranch_lanes = [batch_all(after(cells, leaving[0])) for cells in dbranch_sent]
    waiting = [project_sum, block_output, dbranch_lanes, second_sent[2], second_sent[3]]
    dnormed_one, waiting = lax.optimization_barrier((dnormed_one, waiting))
    project_sum, block_output, dbranch_lanes, second_sent[2], second_sent[3] = waiting
    second_others = [cells for chunk in zip(*second_sent) for cells in chunk]
    dbranch_lane = jnp.concatenate(
        [after(lane_columns(dbranch)[0], dnormed_one)] + dbranch_lanes, axis=0
    )
    second_all = jnp.concatenate([after(second_in, dnormed_one)] + second_others, axis=0)
    narrow_grad = mm(dbranch_lane, second_all, ((0,), (0,))).astype(bf16)
    dpre_lane = jnp.concatenate(
        [after(dpre_cuts[0], narrow_grad)] + dpre_sent, axis=0
    )
    first_all = jnp.concatenate([after(first_in, narrow_grad)] + first_others, axis=0)
    widen_grad = mm(first_all, dpre_lane, ((0,), (0,))).astype(bf16)
    widen_grad = widen_grad.reshape(batch, wide_rows, width)
    widen_pieces = exchange_batch(
        lambda member: lax.dynamic_index_in_dim(widen_grad, member, 0, keepdims=False)
    )
    narrow_sum = over_planes(after(narrow_grad, project_part).reshape(batch, shard, mine))
    dconved = keep_own * row_norm_back(normed_one, inverse_one, after(dnormed_one, widen_grad))
    dconved_low = dconved.astype(bf16)
    for bit in bits_of(batch):
        low = dtext_part.astype(bf16)
        low = after(low, leaving[0] if bit == 1 else dconved_low)
        dtext_part = low.astype(f32) + swap(low, "batch", bit).astype(f32)
    dtext = dtext_part.astype(bf16)

    grad_ext = halo(dconved_low, margin)
    text_cut = [
        jnp.concatenate(
            [dtext[:, (p * ring + g) * shard : (p * ring + g + 1) * shard] for p in range(batch)],
            axis=1,
        )
        for g in range(ring)
    ]
    text_grad = mm(choose(text_cut, lane), soft, ((0,), (0,))).astype(bf16)
    text_pieces = plane_pieces(text_grad.reshape(batch, shard, clip_rows))
    text_bias_part = jnp.sum(dtext.astype(f32), axis=0) * (first_lane * (bi == 0).astype(f32))
    dlatent = dafter
    depth_rows = []
    for tap, (step_row, step_col) in enumerate(taps):
        depth_rows.append(jnp.sum(window(source_ext, step_row, step_col) * dconved, axis=0))
        dlatent = dlatent + window(grad_ext, -step_row, -step_col) * depth_taps[tap]
    latent_grad = turn(dlatent.astype(bf16))
    group_cols = jnp.sum(dqkv_seq.astype(f32), axis=0) + jnp.sum(dtext_low.astype(f32), axis=0)
    shift_part = []
    for third in (0, 2):
        cells = group_cols[third * span : (third + 1) * span]
        cells = [jnp.where(lane == g, cells, jnp.zeros_like(cells)) for g in range(ring)]
        shift_part.append(jnp.concatenate(cells)[:wide_rows])
    pad = max(channels, mine, 2 * wide_rows)

    def line(cells):
        return jnp.pad(cells, (0, pad - cells.shape[0]))

    late = [
        jnp.sum(upstream, axis=0),
        jnp.sum(dbranch_own.astype(f32), axis=0),
        text_bias_part,
        jnp.sum(dconved, axis=0),
    ] + depth_rows
    shared = len(late)
    late = late + [jnp.concatenate(shift_part), widen_bias_part, gain_rows[0], gain_rows[1]]
    sliced = len(late)
    once = first_lane * (bi == 0).astype(f32)
    late = lane_sum(jnp.stack([line(cells) for cells in late + dshift + [time_own[0] * once]]))
    by_plane = [late] + [swap(late, "blk", ring * d) for d in range(1, batch)]
    by_plane[0], *text_pieces = gate(by_plane[0], *text_pieces)
    late = jnp.concatenate(
        [tree_sum([cells[:sliced] for cells in by_plane])] + [cells[sliced:] for cells in by_plane]
    )
    members = gather_batch(late).reshape((batch,) + late.shape)
    both = tree_sum(members)
    widen_held = jnp.stack(widen_pieces)

    def for_plane(member):
        return lax.dynamic_index_in_dim(widen_held, member ^ bi, 0, keepdims=False)

    widen_held = jnp.stack([for_plane(p) for p in range(batch)])
    widen_sum = over_planes(widen_held)
    arrived = grad_ext

    output_bias_sum, narrow_bias_sum, text_bias_sum, depth_bias_sum = (
        both[i, :channels] for i in range(4)
    )
    depth_weight_sum = both[4:shared, :channels]
    shifts = [
        jnp.concatenate([both[sliced + 3 * d, :channels], both[sliced + 3 * d + 1, :channels]])
        for d in range(batch)
    ]
    time_bias_sum = tree_sum(shifts)
    time_weight_sum = tree_sum(
        both[sliced + 3 * d + 2, : time_embed.shape[1]][:, None] * shifts[d][None, :]
        for d in range(batch)
    )
    ordered = jnp.stack(
        [lax.dynamic_index_in_dim(members[:, shared:sliced], l ^ bi, 0, keepdims=False) for l in range(batch)]
    )
    project_bias_sum = jnp.concatenate(
        [
            ordered[:, 0, :wide_rows].reshape(-1),
            ordered[:, 0, wide_rows : 2 * wide_rows].reshape(-1),
        ]
    )
    widen_bias_sum = ordered[:, 1, :mine].reshape(-1)
    gain_sum = jnp.stack([ordered[:, 2, :mine].reshape(-1), ordered[:, 3, :mine].reshape(-1)])

    project_sum = jnp.concatenate([after(project_sum[0], arrived)] + project_sum[1:], axis=1)
    project_sum = project_sum.astype(f32)

    return (
        block_output[None],
        latent_grad[None],
        depth_weight_sum,
        depth_bias_sum,
        widen_sum,
        widen_bias_sum,
        gain_sum,
        after(narrow_sum, arrived).T,
        narrow_bias_sum,
        time_weight_sum,
        time_bias_sum,
        add_up(text_pieces).T,
        text_bias_sum,
        project_sum,
        project_bias_sum,
        after(add_up(output_pieces), arrived).T,
        output_bias_sum,
    )


def solution(mesh):
    rows = P("batch", "blk", None)
    first = P("batch", None)
    both = P("batch", "blk")
    everywhere = P()
    placed = (
        rows,
        first,
        P("batch", None, None),
        first,
        everywhere,
        everywhere,
        first,
        everywhere,
        everywhere,
        first,
        everywhere,
        everywhere,
        everywhere,
        first,
        everywhere,
        first,
        everywhere,
        first,
        everywhere,
        rows,
    )
    given = (
        rows,
        rows,
        everywhere,
        everywhere,
        both,
        everywhere,
        everywhere,
        both,
        everywhere,
        everywhere,
        everywhere,
        both,
        everywhere,
        both,
        everywhere,
        both,
        everywhere,
    )
    return jax.shard_map(
        on_device, mesh=mesh, in_specs=placed, out_specs=given, check_vma=False
    )
```
